512 devices in a mesh: blk: 128 (over y, z, core), sub: 4 (over x).
Axes of the slice: x: 4, y: 8, z: 8, core: 2. Of those that a mesh axis runs over, the one named last changes fastest.
Arguments:
- coords: float32 [3, 524288], P(None, ('blk', 'sub')), may hold values from 0 to 13, as said below
- right_side: float32 [2, 524288], P(None, ('blk', 'sub')), may hold values from -20 to 20
- tile_pairs: int32 [2, 18432], P(None, ('blk', 'sub')), may hold values from 0 to 2047, as said below
- tile_count: int32 [512], P(('blk', 'sub')), may hold values from 1 to 36, as said below
- fine_noise: float32 [2048, 256, 256], P(('blk', 'sub')), may hold values from -0.109375 to 0.109375
- coarse_noise: bfloat16 [1024, 1024], P('sub'), may hold values from -0.0546875 to 0.0546875
- aggregate: int32 [524288], P(('blk', 'sub')), may hold values from 0 to 1023, as said below
Outputs:
- solution_field: float32 [2, 524288], P(None, ('blk', 'sub'))
- residual: float32 [2, 524288], P(None, ('blk', 'sub'))
- direction: float32 [2, 524288], P(None, ('blk', 'sub'))
The draws below stay inside these ranges and needn't reach their ends.
Inputs may be any that keep to these rules, and one draw needn't show every extreme that they name: `coords`: coordinates of the points. `tile_pairs`: global block numbers. A device's pairs have row blocks among its own blocks and column blocks within 4 blocks of the row block. Over all devices the live pairs form a symmetric set with no pair twice, holding every block with itself and with the blocks next to it. Slots past the count hold one of the device's blocks paired with itself. `tile_count`: some device has all 36 slots live in every draw. `aggregate`: point p's centre differs from p // 512 by at most one.
All inputs are finite; a program needn't handle non-finite values.
Results may differ from the reference program's by a relative error of at most 0.00035.
Values sent between devices are 32-bit elements; how exact they have to be, the bound alone decides.
No kernel may reach another device: no remote copies, remote signals or barrier semaphores. Data moves between devices by JAX's collectives and lax.ppermute only.
A program may use at most 64 MiB of HBM per device.

```python
import jax
import jax.numpy as jnp
from jax import lax

BLOCK = 256
REACH = 4
AGG = 512
ITERS = 4
NB_DEV = 16
FIELDS = 2
BLOCKS = 2048
NC = 1024
N_SUB = 4
DEVICES = 512


def draw_coords(key, part):
    points = BLOCKS * BLOCK
    position = jnp.arange(points, dtype=jnp.int32)
    block_id = position // BLOCK
    strip_row = block_id // 64
    along_x = block_id % 64
    along_x = jnp.where(strip_row % 2 == 0, along_x, 63 - along_x)
    jitter = jax.random.uniform(jax.random.fold_in(key, 11), (3, points), jnp.float32)
    xcoord = (along_x.astype(jnp.float32) + jitter[0]) * 0.2
    ycoord = (strip_row.astype(jnp.float32) + jitter[1]) * 0.2
    zcoord = jitter[2] * 0.3
    return jnp.stack([xcoord, ycoord, zcoord])


def draw_right_side(key, part):
    points = BLOCKS * BLOCK
    ramp = jnp.arange(points, dtype=jnp.int32).astype(jnp.float32) / points
    growth = jnp.exp(ramp * jnp.log(3.0))
    values = jnp.clip(jax.random.normal(key, (FIELDS, points), jnp.float32), -6.0, 6.0) * growth
    return values


def tile_layout(key):
    own_blocks = NB_DEV // N_SUB
    devices = BLOCKS // own_blocks
    base_key = jax.random.fold_in(key, 77)
    first_draw = jax.random.randint(jax.random.fold_in(base_key, 1), (devices,), 0, 9)
    second_draw = jax.random.randint(jax.random.fold_in(base_key, 2), (devices,), 0, 9)
    level = 1 + first_draw * second_draw // 9
    chosen = jax.random.randint(jax.random.fold_in(base_key, 3), (), 1, devices - 1)
    level = jnp.where(jnp.arange(devices, dtype=jnp.int32) == chosen, 9, level)
    block_level = jnp.repeat(level, own_blocks, total_repeat_length=BLOCKS)
    coins = jax.random.randint(jax.random.fold_in(base_key, 4), (BLOCKS, REACH), 0, 8)
    row_ids = jnp.arange(BLOCKS, dtype=jnp.int32)
    offsets = jnp.arange(1, REACH + 1, dtype=jnp.int32)
    partner = row_ids[:, None] + offsets[None, :]
    inside = partner < BLOCKS
    partner_safe = jnp.minimum(partner, BLOCKS - 1)
    strength = jnp.maximum(block_level[:, None], block_level[partner_safe])
    forward = inside & ((coins < strength) | (offsets[None, :] == 1))
    source = row_ids[:, None] - offsets[None, :]
    backward = (source >= 0) & forward[jnp.maximum(source, 0), offsets[None, :] - 1]
    present = jnp.concatenate([backward[:, ::-1], jnp.ones((BLOCKS, 1), bool), forward], axis=1)
    spread = jnp.arange(-REACH, REACH + 1, dtype=jnp.int32)
    columns = row_ids[:, None] + spread[None, :]
    rows_grid = jnp.broadcast_to(row_ids[:, None], columns.shape)
    columns = jnp.where(present, columns, rows_grid)
    slot_count = own_blocks * (2 * REACH + 1)
    present_dev = present.reshape(devices, slot_count).astype(jnp.int32)
    sort_key = (1 - present_dev) * slot_count + jnp.arange(slot_count, dtype=jnp.int32)[None, :]
    order = jnp.argsort(sort_key, axis=1, stable=True)
    rows_dev = jnp.take_along_axis(rows_grid.reshape(devices, slot_count), order, axis=1)
    cols_dev = jnp.take_along_axis(columns.reshape(devices, slot_count), order, axis=1)
    counts = jnp.sum(present_dev, axis=1).astype(jnp.int32)
    pairs = jnp.stack([rows_dev.reshape(-1), cols_dev.reshape(-1)]).astype(jnp.int32)
    return (pairs, counts)


def draw_tile_pairs(key, part):
    return tile_layout(key)[0]


def draw_tile_count(key, part):
    return tile_layout(key)[1]


def draw_aggregate(key, part):
    points = BLOCKS * BLOCK
    position = jnp.arange(points, dtype=jnp.int32)
    nudge = jax.random.randint(jax.random.fold_in(key, 5), (points,), -1, 2)
    return jnp.clip(position // AGG + nudge, 0, NC - 1).astype(jnp.int32)


def block_scale(key, extent, cuts, smallest, high):
    gain, own = 1.0, jax.random.fold_in(key, 6)
    for dim, shards_of in cuts:
        draws = jnp.exp(jax.random.uniform(jax.random.fold_in(own, dim), (shards_of,), jnp.float32, smallest / len(cuts), high / len(cuts)))
        gain = gain * jnp.repeat(draws, extent[dim] // shards_of).reshape([-1 if axis == dim else 1 for axis in range(len(extent))])
    return gain


def scatter_about(key, shape, width, most, split=(), kind=jnp.bfloat16):
    factor_of = block_scale(key, shape, split, -0.22, 0.18) if split else 1.0
    drawn = jax.random.normal(key, shape, jnp.float32) * width * factor_of
    return jnp.minimum(jnp.maximum(drawn, -most), most).astype(kind)


def setup_inputs(seed: int = 0) -> dict:
    key_list = jax.random.split(jax.random.key(seed), 8)
    return {
        "coords": draw_coords(jax.random.fold_in(key_list[7], 71), 0),
        "right_side": draw_right_side(jax.random.fold_in(key_list[7], 71), 0),
        "tile_pairs": draw_tile_pairs(jax.random.fold_in(key_list[7], 71), 0),
        "tile_count": draw_tile_count(jax.random.fold_in(key_list[7], 71), 0),
        "fine_noise": scatter_about(key_list[4], (BLOCKS, BLOCK, BLOCK), (0.3 / BLOCK ** 0.5), 0.109375, ((0, 512),), jnp.float32),
        "coarse_noise": scatter_about(key_list[5], (NC, NC), (0.3 / NC ** 0.5), 0.0546875, ((0, 4),)),
        "aggregate": draw_aggregate(jax.random.fold_in(key_list[7], 71), 0),
    }


support_radius = 1.0
diagonal_shift = 1.5
highest = lax.Precision.HIGHEST

def wendland(row_xyz, col_xyz):
    dist_sq = (row_xyz[0][:, :, None] - col_xyz[0][:, None, :]) ** 2
    dist_sq = dist_sq + (row_xyz[1][:, :, None] - col_xyz[1][:, None, :]) ** 2
    dist_sq = dist_sq + (row_xyz[2][:, :, None] - col_xyz[2][:, None, :]) ** 2
    scaled = jnp.sqrt(dist_sq) / support_radius
    falloff = jnp.maximum(1.0 - scaled, 0.0)
    return falloff ** 4 * (4.0 * scaled + 1.0)

def apply_kernel(vector, coords, tile_pairs, tile_count):
    block_total = coords.shape[1] // BLOCK
    xyz_blocks = coords.reshape(3, block_total, BLOCK)
    vec_blocks = vector.reshape(FIELDS, block_total, BLOCK)
    per_device = block_total // DEVICES
    slot_count = tile_pairs.shape[1] // DEVICES
    pair_table = tile_pairs.reshape(2, DEVICES, slot_count).transpose(1, 0, 2)

    def one_device(packed):
        dev_pairs, live_count, device = packed
        row_sel = dev_pairs[0]
        col_sel = dev_pairs[1]
        live_mask = (jnp.arange(slot_count, dtype=jnp.int32) < live_count).astype(jnp.float32)
        kernel_tile = wendland(xyz_blocks[:, row_sel], xyz_blocks[:, col_sel])
        contrib = jnp.einsum('nac,fnc->nfa', kernel_tile, vec_blocks[:, col_sel], precision=highest)
        local_row = row_sel - device * per_device
        row_pick = (local_row[:, None] == jnp.arange(per_device, dtype=jnp.int32)[None, :]).astype(jnp.float32)
        row_pick = row_pick * live_mask[:, None]
        return jnp.einsum('nr,nfa->fra', row_pick, contrib, precision=highest)
    pieces = lax.map(one_device, (pair_table, tile_count, jnp.arange(DEVICES, dtype=jnp.int32)))
    summed = pieces.transpose(1, 0, 2, 3).reshape(FIELDS, block_total * BLOCK)
    kernel_scale = 1.0 / (BLOCK * (2 * REACH + 1))
    return diagonal_shift * vector + summed * kernel_scale

def precondition(residual, fine_noise, coarse_noise, aggregate):
    res_blocks = residual.reshape(FIELDS, -1, BLOCK)
    half_step = res_blocks + jnp.einsum('bac,fbc->fba', fine_noise, res_blocks, precision=highest)
    fine_part = half_step + jnp.einsum('bca,fbc->fba', fine_noise, half_step, precision=highest)
    fine_part = fine_part.reshape(FIELDS, -1)
    centres = coarse_noise.shape[0]
    coarse_res = jax.vmap(lambda values: jax.ops.segment_sum(values, aggregate, centres))(residual)
    coarse_scale = AGG ** (-0.25)
    lifted = coarse_scale * (coarse_res + jnp.dot(coarse_res, coarse_noise.T, precision=highest))
    coarse_sol = coarse_scale * (lifted + jnp.dot(lifted, coarse_noise, precision=highest))
    result = fine_part + jnp.take(coarse_sol, aggregate, axis=1)
    return (result, lax.optimization_barrier(jnp.sum(residual * result, axis=1)))

def reference(coords, right_side, tile_pairs, tile_count, fine_noise, coarse_noise, aggregate):
    coarse_wide = coarse_noise.astype(jnp.float32)
    solution_field = jnp.zeros_like(right_side)
    residual = right_side
    precond, rz_now = precondition(residual, fine_noise, coarse_wide, aggregate)
    direction = precond
    for iteration in range(ITERS):
        image_vec = apply_kernel(direction, coords, tile_pairs, tile_count)
        step_size = rz_now / lax.optimization_barrier(jnp.sum(direction * image_vec, axis=1))
        solution_field = solution_field + step_size[:, None] * direction
        residual = residual - step_size[:, None] * image_vec
        precond, rz_next = precondition(residual, fine_noise, coarse_wide, aggregate)
        direction = precond + (rz_next / rz_now)[:, None] * direction
        rz_now = rz_next
    return (solution_field, residual, direction)
```

```python
import functools

import jax
import jax.numpy as jnp
from jax import lax
from jax.experimental import pallas as pl
from jax.experimental.pallas import tpu as pltpu
from jax.sharding import PartitionSpec as P

BLOCK = 256
REACH = 4
AGG = 512
ITERS = 4
SHIFT = 1.5
KERNEL_SCALE = 1.0 / (BLOCK * (2 * REACH + 1))
OWN = 4
POINTS = OWN * BLOCK
WIN = 3 * POINTS
SPAN = 2 * REACH + 1
HALF = 64
NEAR = 4
COLS = 8
WIDE = 16
AXES = ("blk", "sub")
F32 = jnp.float32
BF16 = jnp.bfloat16
HIGHEST = lax.Precision.HIGHEST
PARAMS = pltpu.CompilerParams(vmem_limit_bytes=24 * 1024 * 1024)


def vmem(count):
    return [pl.BlockSpec(memory_space=pltpu.VMEM)] * count


def call(body, outs, scratch=(), smem=0, **kw):
    def run(*args):
        specs = [pl.BlockSpec(memory_space=pltpu.SMEM)] * smem + vmem(len(args) - smem)
        return pl.pallas_call(
            body,
            out_shape=[jax.ShapeDtypeStruct(s, d) for s, d in outs],
            in_specs=specs,
            out_specs=vmem(len(outs)),
            scratch_shapes=list(scratch),
            compiler_params=PARAMS,
            **kw,
        )(*args)

    return run


def iota(shape, dim):
    return lax.broadcasted_iota(jnp.int32, shape, dim)


def split3(x):
    hi = x.astype(BF16).astype(F32)
    rest = x - hi
    mid = rest.astype(BF16).astype(F32)
    return hi, mid, rest - mid


def stacked(x):
    return jnp.concatenate(split3(x), axis=0).astype(BF16)


def fold(acc):
    return acc[0:2] + acc[2:4] + acc[4:6]


def lane_sum(x):
    return jnp.sum(x, axis=1, keepdims=True)


def fine_apply(vec, f_hi, f_mid, f_lo):
    parts = []
    for b in range(OWN):
        rows = stacked(vec[:, b * BLOCK : (b + 1) * BLOCK])
        acc = jnp.dot(rows, f_hi[b], preferred_element_type=F32)
        acc = acc + jnp.dot(rows, f_mid[b], preferred_element_type=F32)
        acc = acc + jnp.dot(rows, f_lo[b], preferred_element_type=F32)
        parts.append(fold(acc))
    return jnp.concatenate(parts, axis=1)


def payload(out_ref, values):
    lane, row = iota((2, 128), 1), iota((2, 128), 0)
    tile = jnp.zeros((2, 128), F32)
    for slot, value in enumerate(values):
        if value is not None:
            tile = jnp.where(lane == row * HALF + slot, value, tile)
    line = jnp.sum(tile, axis=0, keepdims=True)
    out_ref[...] = jnp.broadcast_to(line, out_ref.shape)


def restrict(vec, near):
    return [lane_sum(jnp.where(near == float(k), vec, 0.0)) for k in range(NEAR)]


def pick(line, slot):
    lane, row = iota((2, 128), 1), iota((2, 128), 0)
    return lane_sum(jnp.where(lane == row * HALF + slot, line, 0.0))


def spread(value):
    lane = iota((1, 128), 1)
    return jnp.where(lane < HALF, value[0:1], value[1:2])


def coarse_values(cr, g_ref):
    lane, row = iota((2, 128), 1), iota((2, 128), 0)
    mine = (lane // HALF) == row
    values = []
    for k in range(COLS):
        line = jnp.sum(cr * g_ref[:, k * 128 : (k + 1) * 128], axis=0, keepdims=True)
        values.append(lane_sum(jnp.where(mine, line, 0.0)))
    return values


def prolong(base, aggs, values):
    for k in range(COLS):
        base = base + jnp.where(aggs == float(k), values[k], 0.0)
    return base


def setup_kernel(place, noise, coarse, res, near, f_hi, f_mid, f_lo, zb, pay, g_part):
    eye = (iota((BLOCK, BLOCK), 0) == iota((BLOCK, BLOCK), 1)).astype(F32)
    for b in range(OWN):
        n = noise[b]
        nt = n.T
        f = jnp.dot(nt, n, precision=HIGHEST, preferred_element_type=F32) + (n + nt) + eye
        hi, mid, lo = split3(f)
        f_hi[b] = hi.astype(BF16)
        f_mid[b] = mid.astype(BF16)
        f_lo[b] = lo.astype(BF16)
    r = res[...]
    zb[...] = fine_apply(r, f_hi, f_mid, f_lo)
    payload(pay, restrict(r, near[...]))
    rows, centres = coarse.shape
    first_col, first_row = place[0], place[1]
    c = coarse[...]
    sel = (iota((WIDE, centres), 1) == first_col + iota((WIDE, centres), 0)).astype(BF16)
    c_sel = lax.dot_general(
        sel, c, (((1,), (1,)), ((), ())), preferred_element_type=F32
    )
    e_sel = (first_row + iota((WIDE, rows), 1) == first_col + iota((WIDE, rows), 0)).astype(F32)
    both = jnp.concatenate([c_sel, e_sel], axis=0).astype(BF16)
    full = jnp.dot(both, c, preferred_element_type=F32)
    g_part[...] = full[:WIDE] + full[WIDE:]
    start = pl.multiple_of(first_row, rows)
    g_part[:, pl.ds(start, rows)] = g_part[:, pl.ds(start, rows)] + (c_sel + e_sel)


def tile_kernel(present, place, xyz, g_sum, k_hi, k_lo, g_lines, tall):
    def one(t, carry):
        i = t // SPAN
        o = t - i * SPAN
        live = present[t]

        @pl.when(live > 0.0)
        def _():
            row = xyz[:, pl.ds(pl.multiple_of((i + REACH) * BLOCK, BLOCK), BLOCK)]
            col = xyz[:, pl.ds(pl.multiple_of((i + o) * BLOCK, BLOCK), BLOCK)].T
            d2 = (col[:, 0:1] - row[0:1]) ** 2
            d2 = d2 + (col[:, 1:2] - row[1:2]) ** 2
            d2 = d2 + (col[:, 2:3] - row[2:3]) ** 2
            dist = d2 * lax.rsqrt(jnp.maximum(d2, 1e-30))
            fall = jnp.maximum(1.0 - dist, 0.0)
            fall = fall * fall
            value = (fall * fall) * (4.0 * dist + 1.0)
            hi = value.astype(BF16)
            k_hi[i, pl.ds(pl.multiple_of(o * BLOCK, BLOCK), BLOCK)] = hi
            k_lo[i, pl.ds(pl.multiple_of(o * BLOCK, BLOCK), BLOCK)] = (
                value - hi.astype(F32)
            ).astype(BF16)

        @pl.when(live <= 0.0)
        def _():
            zero = jnp.zeros((BLOCK, BLOCK), BF16)
            k_hi[i, pl.ds(pl.multiple_of(o * BLOCK, BLOCK), BLOCK)] = zero
            k_lo[i, pl.ds(pl.multiple_of(o * BLOCK, BLOCK), BLOCK)] = zero

        return carry

    lax.fori_loop(0, OWN * SPAN, one, 0)
    centres = g_sum.shape[1]
    devices = centres // 2
    scale = AGG ** (-0.5)
    tall[...] = jnp.zeros_like(tall)
    wide = jnp.concatenate([g_sum[...] * scale, jnp.zeros((128 - WIDE, centres), F32)], axis=0)
    tall[8 : 8 + centres, :] = wide.T
    low = place[2]
    lane = iota((128, COLS * 128), 1)
    src = iota((128, COLS * 128), 0)
    total = jnp.zeros((devices, COLS * 128), F32)
    for slot in range(NEAR):
        rows = tall[pl.ds(7 + slot, devices, stride=2), :]
        perm = (((lane % HALF) == slot) & (src == lane // 128 + low)).astype(BF16)
        for part in split3(rows):
            total = total + jnp.dot(part.astype(BF16), perm, preferred_element_type=F32)
    g_lines[...] = total


def sweep(z_win, k_hi, k_lo):
    rows = stacked(z_win)
    parts = []
    for i in range(OWN):
        lhs = rows[:, i * BLOCK : (i + SPAN) * BLOCK]
        acc = jnp.dot(lhs, k_hi[i], preferred_element_type=F32)
        acc = acc + jnp.dot(lhs, k_lo[i], preferred_element_type=F32)
        parts.append(fold(acc))
    own = z_win[:, POINTS : 2 * POINTS]
    return SHIFT * own + KERNEL_SCALE * jnp.concatenate(parts, axis=1)


def first_kernel(
    gath, g_lines, zb, aggs, res, near, k_hi, k_lo, f_hi, f_mid, f_lo, z_out, w_out, mw_out, pay
):
    z_win = prolong(zb[...], aggs[...], coarse_values(gath[...], g_lines))
    z = z_win[:, POINTS : 2 * POINTS]
    w = sweep(z_win, k_hi, k_lo)
    z_out[...] = z
    w_out[...] = w
    mw_out[...] = fine_apply(w, f_hi, f_mid, f_lo)
    dots = [lane_sum(res[...] * z), lane_sum(z * w)]
    payload(pay, restrict(w, near[...]) + dots)


def step_kernel(first, last, *refs):
    it = iter(refs)
    take = lambda n: [next(it) for _ in range(n)]
    gath, g_lines, aggs, near = take(4)
    k_hi, k_lo, f_hi, f_mid, f_lo = (None,) * 5
    if not last:
        k_hi, k_lo, f_hi, f_mid, f_lo = take(5)
    x, r, z, w, cr, zb = take(6)
    mw_refs = take(1 if last else 3)
    d_old = q_old = crq_old = mq_old = rz_old = curve_old = None
    if not first:
        d_old, q_old, crq_old, mq_old, rz_old, curve_old = take(6)
    if last:
        x_out, r_out, z_out, d_out, rz_out, pay = take(6)
    else:
        x_out, r_out, z_out, w_out, cr_out, zb_out, mw_out = take(7)
        d_out, q_out, crq_out, mq_out, rz_out, curve_out, pay = take(7)

    got = gath[...]
    total = jnp.sum(got, axis=0, keepdims=True)
    rz, zw = pick(total, NEAR), pick(total, NEAR + 1)
    mw = jnp.concatenate([ref[...] for ref in mw_refs], axis=1)
    mid = slice(POINTS, 2 * POINTS)
    if first:
        curve = zw
        d, q, crq, mq = z[...], w[...], got, mw
    else:
        zq = pick(total, NEAR + 2)
        beta = rz / rz_old[:, 0:1]
        curve = zw + beta * (2.0 * zq + beta * curve_old[:, 0:1])
        d = z[...] + beta * d_old[...]
        q = w[...] + beta * q_old[...]
        crq = got + spread(beta) * crq_old[...]
        mq = mw + beta * (mq_old[:, mid] if last else mq_old[...])
    alpha = rz / curve
    r_new = r[...] - alpha * q
    x_out[...] = alpha * d if first else x[...] + alpha * d
    r_out[...] = r_new
    d_out[...] = d
    rz_out[...] = jnp.broadcast_to(rz, rz_out.shape)
    cr_new = cr[...] - spread(alpha) * crq
    zb_new = (zb[:, mid] if last else zb[...]) - alpha * mq
    values = coarse_values(cr_new, g_lines)
    if last:
        z_new = prolong(zb_new, aggs[:, mid], values)
        z_out[...] = z_new
        payload(pay, [None] * NEAR + [lane_sum(r_new * z_new)])
        return
    z_win = prolong(zb_new, aggs[...], values)
    z_new = z_win[:, POINTS : 2 * POINTS]
    w_new = sweep(z_win, k_hi, k_lo)
    z_out[...] = z_new
    w_out[...] = w_new
    cr_out[...] = cr_new
    zb_out[...] = zb_new
    q_out[...] = q
    crq_out[...] = crq
    mq_out[...] = mq
    curve_out[...] = jnp.broadcast_to(curve, curve_out.shape)
    mw_out[...] = fine_apply(w_new, f_hi, f_mid, f_lo)
    dots = [lane_sum(r_new * z_new), lane_sum(z_new * w_new), lane_sum(z_new * q)]
    payload(pay, restrict(w_new, near[...]) + dots)


def last_kernel(gath, z, d_old, rz_old, d_out):
    total = jnp.sum(gath[...], axis=0, keepdims=True)
    beta = pick(total, NEAR) / rz_old[:, 0:1]
    d_out[...] = z[...] + beta * d_old[...]


def halo(block):
    count = lax.axis_size(AXES)
    forward = [(i, i + 1) for i in range(count - 1)]
    backward = [(i + 1, i) for i in range(count - 1)]
    return lax.ppermute(block, AXES, forward), lax.ppermute(block, AXES, backward)


def exchange(rows):
    return lax.all_to_all(rows, AXES, 0, 0, tiled=True)


def per_device(coords, right_side, tile_pairs, tile_count, fine_noise, coarse_noise, aggregate):
    fields = right_side.shape[0]
    devices = lax.axis_size(AXES)
    centres = coarse_noise.shape[1]
    group, part = lax.axis_index("blk"), lax.axis_index("sub")
    subs = lax.axis_size("sub")
    device = group * subs + part
    rows = coarse_noise.shape[0]
    vec, win = (fields, POINTS), (fields, WIN)
    line, small = (devices, 128), (fields, 128)
    tiles = (OWN, SPAN * BLOCK, BLOCK)
    fines = (OWN, BLOCK, BLOCK)

    slots = tile_pairs.shape[1]
    live = jnp.arange(slots, dtype=jnp.int32) < tile_count[0]
    place_of = (tile_pairs[0] - device * OWN) * SPAN + (tile_pairs[1] - tile_pairs[0] + REACH)
    spots = jnp.arange(OWN * SPAN, dtype=jnp.int32)
    hit = (place_of[None, :] == spots[:, None]) & live[None, :]
    present = jnp.max(hit.astype(F32), axis=1)

    place = jnp.stack([group * subs * 2 - 4, part * rows, 2 * part + 1]).astype(jnp.int32)
    agg_line = aggregate.astype(F32)[None]
    near = agg_line - (2 * device - 1).astype(F32)
    f_hi, f_mid, f_lo, zb, pay, g_part = call(
        setup_kernel,
        [(fines, BF16)] * 3 + [(vec, F32), (line, F32), ((WIDE, centres), F32)],
        smem=1,
    )(place, fine_noise, coarse_noise, right_side, near)

    mine = jnp.concatenate([coords, agg_line, zb, jnp.zeros((2, POINTS), F32)], axis=0)
    left, right = halo(mine)
    g_sum = lax.psum(g_part, "sub")
    got = exchange(pay)
    window = jnp.concatenate([left, mine, right], axis=1)
    k_hi, k_lo, g_lines = call(
        tile_kernel,
        [(tiles, BF16), (tiles, BF16), ((devices, COLS * 128), F32)],
        scratch=[pltpu.VMEM((centres + 16, 128), F32)],
        smem=2,
    )(present, place, window, g_sum)
    aggs = window[3:4] - (2 * device - 3).astype(F32)
    zb = window[4:6]
    kernels = (k_hi, k_lo, f_hi, f_mid, f_lo)

    z, w, mw, pay = call(
        first_kernel, [(vec, F32), (vec, F32), (vec, F32), (line, F32)]
    )(got, g_lines, zb, aggs, right_side, near, *kernels)
    x, r, cr = right_side, right_side, got
    old = ()
    for iteration in range(ITERS):
        first, last = iteration == 0, iteration == ITERS - 1
        if last:
            mws = (mw,)
        else:
            mw_l, mw_r = halo(mw)
            mws = (mw_l, mw, mw_r)
        got = exchange(pay)
        args = (got, g_lines, aggs, near) + (() if last else kernels)
        args = args + (x, r, z, w, cr, zb) + mws + old
        body = functools.partial(step_kernel, first, last)
        if last:
            outs = [(vec, F32)] * 4 + [(small, F32), (line, F32)]
            x, r, z, d, rz, pay = call(body, outs)(*args)
        else:
            outs = [(vec, F32)] * 4 + [(line, F32), (win, F32), (vec, F32)]
            outs = outs + [(vec, F32)] * 2 + [(line, F32), (win, F32)]
            outs = outs + [(small, F32)] * 2 + [(line, F32)]
            x, r, z, w, cr, zb, mw, d, q, crq, mq, rz, curve, pay = call(body, outs)(*args)
            old = (d, q, crq, mq, rz, curve)
    got = exchange(pay)
    (d,) = call(last_kernel, [(vec, F32)])(got, z, d, rz)
    return (x, r, d)


def solution(mesh):
    in_specs = (
        P(None, AXES),
        P(None, AXES),
        P(None, AXES),
        P(AXES),
        P(AXES, None, None),
        P("sub", None),
        P(AXES),
    )
    out_specs = (P(None, AXES), P(None, AXES), P(None, AXES))
    return jax.shard_map(
        per_device, mesh=mesh, in_specs=in_specs, out_specs=out_specs, check_vma=False
    )
```

```python
import functools

import jax
import jax.numpy as jnp
from jax import lax
from jax.experimental import pallas as pl
from jax.experimental.pallas import tpu as pltpu
from jax.sharding import Mesh
from jax.sharding import PartitionSpec as P

BLOCK = 256
REACH = 4
AGG = 512
ITERS = 4
SHIFT = 1.5
KERNEL_SCALE = 1.0 / (BLOCK * (2 * REACH + 1))
OWN = 4
POINTS = OWN * BLOCK
WIN = 3 * POINTS
MID = slice(POINTS, 2 * POINTS)
SPAN = 2 * REACH + 1
HALF = 64
DOTS = 32
NEAR = 4
COLS = 8
WIDE = 16
CORES = 2
AXES = ("grp", "core", "sub")
F32 = jnp.float32
BF16 = jnp.bfloat16
HIGHEST = lax.Precision.HIGHEST


class Arrived:
    def __init__(self, copy, ref):
        self.copy, self.ref, self.done = copy, ref, False

    def __call__(self):
        if not self.done:
            self.copy.wait()
            self.done = True
        return self.ref


class Leaving:
    def __init__(self, copy, ref):
        self.copy, self.ref = copy, ref

    def put(self, value):
        self.ref[...] = value
        self.copy.start()

    def go(self):
        self.copy.start()


def call(body, outs, raw=(), raw_outs=(), scratch=(), smem=0):
    def run(*args):
        ins = args[smem:]
        n, m = len(ins), len(outs)
        p, q = len(raw), len(raw_outs)

        def kernel(*refs):
            refs = list(refs)
            take = lambda k: [refs.pop(0) for _ in range(k)]
            scalars, src, raw_in = take(smem), take(n), take(p)
            dst, raw_out = take(m), take(q)
            v_in, v_out = take(n), take(m)
            sem_in, sem_out = take(2)
            arriving = []
            for i in range(n):
                copy = pltpu.make_async_copy(src[i], v_in[i], sem_in.at[i])
                copy.start()
                arriving.append(Arrived(copy, v_in[i]))
            leaving = [
                Leaving(pltpu.make_async_copy(v_out[i], dst[i], sem_out.at[i]), v_out[i])
                for i in range(m)
            ]
            body(*scalars, arriving, leaving, *raw_in, *raw_out, *refs)
            for item in arriving:
                item()
            for item in leaving:
                item.copy.wait()

        shapes = [pltpu.VMEM(a.shape, a.dtype) for a in ins]
        shapes = shapes + [pltpu.VMEM(s, d) for s, d in outs]
        sems = [pltpu.SemaphoreType.DMA((n,)), pltpu.SemaphoreType.DMA((m,))]
        smem_spec = pl.BlockSpec(memory_space=pltpu.SMEM)
        any_spec = pl.BlockSpec(memory_space=pl.ANY)
        return pl.pallas_call(
            kernel,
            out_shape=[jax.ShapeDtypeStruct(s, d) for s, d in list(outs) + list(raw_outs)],
            in_specs=[smem_spec] * smem + [any_spec] * (n + p),
            out_specs=[any_spec] * (m + q),
            scratch_shapes=shapes + sems + list(scratch),
        )(*args, *raw)

    return run


def iota(shape, dim):
    return lax.broadcasted_iota(jnp.int32, shape, dim)


def split2(x):
    hi = x.astype(BF16)
    return hi, (x - hi.astype(F32)).astype(BF16)


def stacked(x):
    hi = x.astype(BF16).astype(F32)
    rest = x - hi
    mid = rest.astype(BF16).astype(F32)
    return jnp.concatenate([hi, mid, rest - mid], axis=0).astype(BF16)


def fold(acc):
    return acc[0:2] + acc[2:4] + acc[4:6]


def lane_sum(x):
    return jnp.sum(x, axis=1, keepdims=True)


def fine_apply(vec, fine):
    rows = stacked(vec)
    parts = []
    for b in range(OWN):
        lhs = rows[:, b * BLOCK : (b + 1) * BLOCK]
        acc = jnp.dot(lhs, fine[b, 0], preferred_element_type=F32)
        acc = acc + jnp.dot(lhs, fine[b, 1], preferred_element_type=F32)
        parts.append(fold(acc))
    return vec + jnp.concatenate(parts, axis=1)


def payload(out, base, coarse, dots):
    lane, row = iota((2, 128), 1), iota((2, 128), 0)
    tile = jnp.zeros((2, 128), F32)
    for slot, value in enumerate(coarse):
        tile = jnp.where(lane == row * HALF + base + slot, value, tile)
    for slot, value in enumerate(dots):
        tile = jnp.where(lane == row * HALF + DOTS + slot, value, tile)
    line = jnp.sum(tile, axis=0, keepdims=True)
    out.put(jnp.broadcast_to(line, out.ref.shape))


def restrict(vec, near):
    return [lane_sum(jnp.where(near == float(k), vec, 0.0)) for k in range(NEAR)]


def pick(line, slot):
    lane, row = iota((2, 128), 1), iota((2, 128), 0)
    return lane_sum(jnp.where(lane == row * HALF + DOTS + slot, line, 0.0))


def spread(value):
    return jnp.where(iota((1, 128), 1) < HALF, value[0:1], value[1:2])


def coarse_values(cr_ref, g_ref):
    acc = [jnp.zeros((COLS, 128), F32) for _ in range(4)]
    for g in range(cr_ref.shape[0]):
        acc[g % 4] = acc[g % 4] + g_ref[:, g * 128 : (g + 1) * 128] * cr_ref[g : g + 1, :]
    total = (acc[0] + acc[1]) + (acc[2] + acc[3])
    first = iota((COLS, 128), 1) < HALF
    return lane_sum(jnp.where(first, total, 0.0)), lane_sum(jnp.where(first, 0.0, total))


def prolong(base, aggs, values):
    for k in range(COLS):
        value = jnp.concatenate([v[k : k + 1] for v in values], axis=0)
        base = base + jnp.where(aggs == float(k), value, 0.0)
    return base


def sweep(z_win, tiles, rows_ref, sum_ref):
    src, k_ref, sem = tiles
    rows_ref[...] = stacked(z_win)

    def one(i, carry):
        pltpu.make_async_copy(src.at[i], k_ref.at[i], sem.at[i]).wait()
        at = pl.multiple_of(i * BLOCK, BLOCK)
        lhs = rows_ref[:, pl.ds(at, SPAN * BLOCK)]
        acc = jnp.dot(lhs, k_ref[i, 0], preferred_element_type=F32)
        acc = acc + jnp.dot(lhs, k_ref[i, 1], preferred_element_type=F32)
        sum_ref[:, pl.ds(at, BLOCK)] = fold(acc)
        return carry

    lax.fori_loop(0, OWN, one, 0)
    return SHIFT * z_win[:, MID] + KERNEL_SCALE * sum_ref[...]


def start_tiles(tiles):
    src, k_ref, sem = tiles
    for i in range(OWN):
        pltpu.make_async_copy(src.at[i], k_ref.at[i], sem.at[i]).start()


def setup_kernel(subs, me, ins, outs):
    res, agg, coarse, coords, noise = ins
    pay, g_part, mine, fine = outs
    device = me[0]
    lane_base = 2 * (device % (CORES * subs))
    r = res()[...]
    agg_line = agg()[...].astype(F32)
    near = agg_line - (2 * device - 1).astype(F32)
    payload(pay, lane_base, restrict(r, near), [])
    rows, centres = coarse.ref.shape
    first_col = device // subs * (2 * subs) - 4
    first_row = device % subs * rows
    c = coarse()[...]
    sel = (iota((WIDE, centres), 1) == first_col + iota((WIDE, centres), 0)).astype(BF16)
    c_sel = lax.dot_general(sel, c, (((1,), (1,)), ((), ())), preferred_element_type=F32)
    e_sel = (first_row + iota((WIDE, rows), 1) == first_col + iota((WIDE, rows), 0)).astype(F32)
    both = jnp.concatenate([c_sel, e_sel], axis=0).astype(BF16)
    full = jnp.dot(both, c, preferred_element_type=F32)
    full = full[:WIDE] + full[WIDE:]
    extra = c_sel + e_sel
    start = pl.multiple_of(first_row, rows)
    for to in range(subs):
        low = 2 * to + 1
        g_part.ref[to] = full[low : low + COLS]
        spot = g_part.ref[to, :, pl.ds(start, rows)]
        g_part.ref[to, :, pl.ds(start, rows)] = spot + extra[low : low + COLS]
    g_part.go()
    noise()
    for b in range(OWN):
        n = noise.ref[b]
        nt = n.T
        f = jnp.dot(nt, n, precision=HIGHEST, preferred_element_type=F32) + (n + nt)
        fine.ref[b, 0], fine.ref[b, 1] = split2(f)
    fine.go()
    mine.ref[0:3] = coords()[...]
    mine.ref[3:4] = agg_line
    mine.ref[4:6] = fine_apply(r, fine.ref)
    mine.ref[6:8] = jnp.zeros((2, POINTS), F32)
    mine.go()


def tile_kernel(subs, me, pairs, live_count, ins, outs, k_out, k_ref, xyz, tall, present, k_sem):
    own, near_a, near_b, parts = ins
    aggs, zb, g_lines = outs
    device = me[0]

    def clear(t, carry):
        present[t] = 0
        return carry

    def mark(s, carry):
        row, col = pairs[0, s], pairs[1, s]
        present[(row - device * OWN) * SPAN + (col - row + REACH)] = 1
        return carry

    lax.fori_loop(0, OWN * SPAN, clear, 0)
    lax.fori_loop(0, live_count[0], mark, 0)
    odd = device % 2 == 1
    a, b = near_a()[...], near_b()[...]
    xyz[:, 0:POINTS] = jnp.where(odd, a, b)
    xyz[:, MID] = own()[...]
    xyz[:, 2 * POINTS : WIN] = jnp.where(odd, b, a)
    aggs.put(xyz[3:4] - (2 * device - 3).astype(F32))
    zb.put(xyz[4:6])

    def one(t, carry):
        i = t // SPAN
        o = t - i * SPAN
        live = present[t]
        spot = pl.ds(pl.multiple_of(o * BLOCK, BLOCK), BLOCK)

        @pl.when(live > 0)
        def _():
            row = xyz[:, pl.ds(pl.multiple_of((i + REACH) * BLOCK, BLOCK), BLOCK)]
            col = xyz[:, pl.ds(pl.multiple_of((i + o) * BLOCK, BLOCK), BLOCK)].T
            d2 = (col[:, 0:1] - row[0:1]) ** 2
            d2 = d2 + (col[:, 1:2] - row[1:2]) ** 2
            d2 = d2 + (col[:, 2:3] - row[2:3]) ** 2
            dist = d2 * lax.rsqrt(jnp.maximum(d2, 1e-30))
            fall = jnp.maximum(1.0 - dist, 0.0)
            fall = fall * fall
            hi, lo = split2((fall * fall) * (4.0 * dist + 1.0))
            k_ref[i, 0, spot] = hi
            k_ref[i, 1, spot] = lo

        @pl.when(live == 0)
        def _():
            zero = jnp.zeros((BLOCK, BLOCK), BF16)
            k_ref[i, 0, spot] = zero
            k_ref[i, 1, spot] = zero

        @pl.when(o == SPAN - 1)
        def _():
            pltpu.make_async_copy(k_ref.at[i], k_out.at[i], k_sem.at[i]).start()

        return carry

    lax.fori_loop(0, OWN * SPAN, one, 0)
    total = parts()[0]
    for s in range(1, subs):
        total = total + parts.ref[s]
    centres = total.shape[1]
    zero = jnp.zeros((COLS, 128), F32)
    tall[:, 0:128] = zero
    tall[:, 128 : 128 + centres] = total * (AGG ** (-0.5))
    tall[:, 128 + centres : 256 + centres] = zero
    lane = iota((COLS, 128), 1)
    step = 2 * CORES * subs
    count = step + 2
    for g in range(centres // step):
        at = 128 + step * g - 1
        lo, off = at // 128 * 128, at % 128
        line = tall[:, lo : lo + 128]
        if off:
            line = pltpu.roll(line, 128 - off, 1)
        if off + count > 128:
            after = pltpu.roll(tall[:, lo + 128 : lo + 256], 128 - off, 1)
            line = jnp.where(lane < 128 - off, line, after)
        line = jnp.where(lane < count, line, 0.0)
        g_lines.ref[:, g * 128 : (g + 1) * 128] = line + pltpu.roll(line, HALF, 1)
    g_lines.go()
    for i in range(OWN):
        pltpu.make_async_copy(k_ref.at[i], k_out.at[i], k_sem.at[i]).wait()


def first_kernel(subs, me, ins, outs, k_src, k_ref, rows_ref, sum_ref, k_sem):
    gath, g_lines, zb, aggs, res, fine = ins
    z_out, w_out, pay, mw_out = outs
    tiles = (k_src, k_ref, k_sem)
    start_tiles(tiles)
    device = me[0]
    gath(), g_lines()
    z_win = prolong(zb()[...], aggs()[...], coarse_values(gath.ref, g_lines.ref))
    z = z_win[:, MID]
    z_out.put(z)
    w = sweep(z_win, tiles, rows_ref, sum_ref)
    w_out.put(w)
    mw_out.put(fine_apply(w, fine()))
    near = aggs.ref[:, MID] - 2.0
    dots = [lane_sum(res()[...] * z), lane_sum(z * w)]
    payload(pay, 2 * (device % (CORES * subs)), restrict(w, near), dots)


def step_kernel(subs, first, last, me, ins, outs, *raw):
    ins, outs = list(ins), list(outs)
    device = me[0]
    take = lambda k: [ins.pop(0) for _ in range(k)]
    give = lambda k: [outs.pop(0) for _ in range(k)]
    gath, z, w, x, r, cr, mw_o, zb, aggs, g_lines = take(10)
    near_mw = [] if last else take(2)
    d_old = q_old = crq_old = mq_old = rz_old = curve_old = None
    if not first:
        rz_old, curve_old, d_old, q_old, crq_old, mq_old = take(6)
    if last:
        x_out, r_out, d_out, z_out, rz_out, pay = give(6)
    else:
        x_out, r_out, d_out, q_out, rz_out, curve_out, crq_out, mq_out = give(8)
        cr_out, zb_out, z_out, w_out, mw_out, pay = give(6)
        (fine,) = take(1)
        k_src, k_ref, rows_ref, sum_ref, k_sem = raw
        tiles = (k_src, k_ref, k_sem)
        start_tiles(tiles)

    got = gath()[...]
    total = jnp.sum(got, axis=0, keepdims=True)
    rz, zw = pick(total, 0), pick(total, 1)
    mw = mw_o()[...]
    if not last:
        odd = device % 2 == 1
        a, b = [item()[...] for item in near_mw]
        mw = jnp.concatenate([jnp.where(odd, a, b), mw, jnp.where(odd, b, a)], axis=1)
    if first:
        curve = zw
        d, q, crq, mq = z()[...], w()[...], got, mw
    else:
        beta = rz / rz_old()[:, 0:1]
        curve = zw + beta * (2.0 * pick(total, 2) + beta * curve_old()[:, 0:1])
        d = z()[...] + beta * d_old()[...]
        q = w()[...] + beta * q_old()[...]
        crq = got + spread(beta) * crq_old()[...]
        mq = mw + beta * (mq_old()[:, MID] if last else mq_old()[...])
    alpha = rz / curve
    r_new = r()[...] - alpha * q
    x_out.put(alpha * d if first else x()[...] + alpha * d)
    r_out.put(r_new)
    d_out.put(d)
    rz_out.put(jnp.broadcast_to(rz, rz_out.ref.shape))
    cr_new = cr()[...] - spread(alpha) * crq
    zb_new = (zb()[:, MID] if last else zb()[...]) - alpha * mq
    cr.ref[...] = cr_new
    values = coarse_values(cr.ref, g_lines())
    if last:
        z_new = prolong(zb_new, aggs()[:, MID], values)
        z_out.put(z_new)
        payload(pay, 0, [], [lane_sum(r_new * z_new)])
        return
    cr_out.put(cr_new)
    zb_out.put(zb_new)
    q_out.put(q)
    crq_out.put(crq)
    mq_out.put(mq)
    curve_out.put(jnp.broadcast_to(curve, curve_out.ref.shape))
    z_win = prolong(zb_new, aggs()[...], values)
    z_new = z_win[:, MID]
    z_out.put(z_new)
    w_new = sweep(z_win, tiles, rows_ref, sum_ref)
    w_out.put(w_new)
    mw_out.put(fine_apply(w_new, fine()))
    dots = [lane_sum(r_new * z_new), lane_sum(z_new * w_new), lane_sum(z_new * q)]
    near = aggs.ref[:, MID] - 2.0
    payload(pay, 2 * (device % (CORES * subs)), restrict(w_new, near), dots)


def last_kernel(ins, outs):
    gath, z, d_old, rz_old = ins
    (d_out,) = outs
    total = jnp.sum(gath()[...], axis=0, keepdims=True)
    beta = pick(total, 0) / rz_old()[:, 0:1]
    d_out.put(z()[...] + beta * d_old()[...])


def neighbours(block):
    count = lax.axis_size(AXES)
    inner = [(i, i ^ 1) for i in range(count)]
    outer = [(i, i + 1) for i in range(1, count - 1, 2)]
    outer = outer + [(i + 1, i) for i in range(1, count - 1, 2)]
    return lax.ppermute(block, AXES, inner), lax.ppermute(block, AXES, outer)


def exchange(rows):
    near = lax.all_to_all(rows, ("core", "sub"), 0, 0, tiled=True)
    groups = lax.axis_size("grp")
    total = jnp.broadcast_to(jnp.sum(near, axis=0, keepdims=True), (groups, 128))
    return lax.all_to_all(total, "grp", 0, 0, tiled=True)


def per_device(coords, right_side, tile_pairs, tile_count, fine_noise, coarse_noise, aggregate):
    fields = right_side.shape[0]
    subs, groups = lax.axis_size("sub"), lax.axis_size("grp")
    centres = coarse_noise.shape[1]
    device = (lax.axis_index("grp") * CORES + lax.axis_index("core")) * subs
    me = jnp.full((1,), device + lax.axis_index("sub"), jnp.int32)
    vec, win = ((fields, POINTS), F32), ((fields, WIN), F32)
    line, small = ((groups, 128), F32), ((fields, 128), F32)
    row = ((CORES * subs, 128), F32)
    tiles = ((OWN, 2, SPAN * BLOCK, BLOCK), BF16)
    fines = ((OWN, 2, BLOCK, BLOCK), BF16)
    lines = ((COLS, groups * 128), F32)
    sweeping = [
        pltpu.VMEM(*tiles),
        pltpu.VMEM((3 * fields, WIN), BF16),
        pltpu.VMEM(*vec),
        pltpu.SemaphoreType.DMA((OWN,)),
    ]

    pay, g_part, mine, fine = call(
        functools.partial(setup_kernel, subs),
        [row, ((subs, COLS, centres), F32), ((8, POINTS), F32), fines],
        smem=1,
    )(me, right_side, aggregate[None], coarse_noise, coords, fine_noise)
    near_a, near_b = neighbours(mine)
    parts = lax.all_to_all(g_part, "sub", 0, 0, tiled=True)
    got = exchange(pay)
    aggs, zb, g_lines, kernel_tiles = call(
        functools.partial(tile_kernel, subs),
        [((1, WIN), F32), win, lines],
        raw_outs=[tiles],
        scratch=[
            pltpu.VMEM(*tiles),
            pltpu.VMEM((8, WIN), F32),
            pltpu.VMEM((COLS, centres + 256), F32),
            pltpu.SMEM((OWN * SPAN,), jnp.int32),
            pltpu.SemaphoreType.DMA((OWN,)),
        ],
        smem=3,
    )(me, tile_pairs, tile_count, mine, near_a, near_b, parts)

    z, w, pay, mw = call(
        functools.partial(first_kernel, subs),
        [vec, vec, row, vec],
        raw=[kernel_tiles],
        scratch=sweeping,
        smem=1,
    )(me, got, g_lines, zb, aggs, right_side, fine)
    x, r, cr = right_side, right_side, got
    old = ()
    for iteration in range(ITERS):
        first, last = iteration == 0, iteration == ITERS - 1
        got = exchange(pay)
        args = (me, got, z, w, x, r, cr, mw, zb, aggs, g_lines)
        args = args + (() if last else neighbours(mw)) + old
        body = functools.partial(step_kernel, subs, first, last)
        if last:
            outs = [vec, vec, vec, vec, small, row]
            x, r, d, z, rz, pay = call(body, outs, smem=1)(*args)
        else:
            outs = [vec] * 4 + [small, small, line, win, line, win, vec, vec, vec, row]
            run = call(body, outs, raw=[kernel_tiles], scratch=sweeping, smem=1)
            x, r, d, q, rz, curve, crq, mq, cr, zb, z, w, mw, pay = run(*args, fine)
            old = (rz, curve, d, q, crq, mq)
    got = exchange(pay)
    (d,) = call(last_kernel, [vec])(got, z, d, rz)
    return (x, r, d)


def solution(mesh):
    devices = mesh.devices
    blk, subs = devices.shape
    fine_mesh = Mesh(devices.reshape(blk // CORES, CORES, subs), AXES)
    points = P(None, AXES)
    in_specs = (
        points,
        points,
        points,
        P(AXES),
        P(AXES, None, None),
        P("sub", None),
        P(AXES),
    )
    return jax.shard_map(
        per_device, mesh=fine_mesh, in_specs=in_specs, out_specs=(points,) * 3, check_vma=False
    )
```

```python
import functools

import jax
import jax.numpy as jnp
from jax import lax
from jax.experimental import pallas as pl
from jax.experimental.pallas import tpu as pltpu
from jax.sharding import Mesh
from jax.sharding import PartitionSpec as P

BLOCK = 256
REACH = 4
AGG = 512
ITERS = 4
SHIFT = 1.5
KERNEL_SCALE = 1.0 / (BLOCK * (2 * REACH + 1))
OWN = 4
POINTS = OWN * BLOCK
WIN = 3 * POINTS
MID = slice(POINTS, 2 * POINTS)
SPAN = 2 * REACH + 1
HALF = 64
DOTS = 32
NEAR = 4
COLS = 8
WIDE = 32
CORES = 2
AXES = ("grp", "core", "sub")
VMEM_LIMIT = 48 * 1024 * 1024
F32 = jnp.float32
BF16 = jnp.bfloat16
HIGHEST = lax.Precision.HIGHEST


class Operand:
    def __init__(self, ref):
        self.ref = ref

    def __call__(self):
        return self.ref

    def put(self, value):
        self.ref[...] = value


def call(body, outs, raw=(), raw_outs=(), scratch=(), smem=0):
    def run(*args):
        n, m = len(args) - smem, len(outs)
        p, q = len(raw), len(raw_outs)

        def kernel(*refs):
            refs = list(refs)
            take = lambda k: [refs.pop(0) for _ in range(k)]
            scalars, ins, raw_in = take(smem), take(n), take(p)
            results, raw_out = take(m), take(q)
            body(
                *scalars,
                [Operand(ref) for ref in ins],
                [Operand(ref) for ref in results],
                *raw_in,
                *raw_out,
                *refs,
            )

        smem_spec = pl.BlockSpec(memory_space=pltpu.SMEM)
        vmem_spec = pl.BlockSpec(memory_space=pltpu.VMEM)
        hbm_spec = pl.BlockSpec(memory_space=pltpu.HBM)
        return pl.pallas_call(
            kernel,
            out_shape=[jax.ShapeDtypeStruct(s, d) for s, d in list(outs) + list(raw_outs)],
            in_specs=[smem_spec] * smem + [vmem_spec] * n + [hbm_spec] * p,
            out_specs=[vmem_spec] * m + [hbm_spec] * q,
            scratch_shapes=list(scratch),
            compiler_params=pltpu.CompilerParams(vmem_limit_bytes=VMEM_LIMIT),
        )(*args, *raw)

    return run


def iota(shape, dim):
    return lax.broadcasted_iota(jnp.int32, shape, dim)


def split2(x):
    hi = x.astype(BF16)
    return hi, (x - hi.astype(F32)).astype(BF16)


def stacked(x):
    hi = x.astype(BF16).astype(F32)
    rest = x - hi
    mid = rest.astype(BF16).astype(F32)
    return jnp.concatenate([hi, mid, rest - mid], axis=0).astype(BF16)


def fold(acc):
    return acc[0:2] + acc[2:4] + acc[4:6]


def lane_sum(x):
    return jnp.sum(x, axis=1, keepdims=True)


def fine_apply(vec, fine):
    rows = stacked(vec)
    parts = []
    for b in range(OWN):
        lhs = rows[:, b * BLOCK : (b + 1) * BLOCK]
        acc = jnp.dot(lhs, fine[b, 0], preferred_element_type=F32)
        acc = acc + jnp.dot(lhs, fine[b, 1], preferred_element_type=F32)
        parts.append(fold(acc))
    return vec + jnp.concatenate(parts, axis=1)


def payload_line(base, coarse, dots):
    lane, row = iota((2, 128), 1), iota((2, 128), 0)
    tile = jnp.zeros((2, 128), F32)
    for slot, value in enumerate(coarse):
        tile = jnp.where(lane == row * HALF + base + slot, value, tile)
    for slot, value in enumerate(dots):
        tile = jnp.where(lane == row * HALF + DOTS + slot, value, tile)
    return jnp.sum(tile, axis=0, keepdims=True)


def payload(out, base, coarse, dots):
    out.put(jnp.broadcast_to(payload_line(base, coarse, dots), out.ref.shape))


def restrict(vec, near):
    return [lane_sum(jnp.where(near == float(k), vec, 0.0)) for k in range(NEAR)]


def pick(line, slot):
    lane, row = iota((2, 128), 1), iota((2, 128), 0)
    return lane_sum(jnp.where(lane == row * HALF + DOTS + slot, line, 0.0))


def spread(value):
    return jnp.where(iota((1, 128), 1) < HALF, value[0:1], value[1:2])


def coarse_values(cr_ref, g_ref):
    acc = [jnp.zeros((COLS, 128), F32) for _ in range(4)]
    for g in range(cr_ref.shape[0]):
        acc[g % 4] = acc[g % 4] + g_ref[:, g * 128 : (g + 1) * 128] * cr_ref[g : g + 1, :]
    total = (acc[0] + acc[1]) + (acc[2] + acc[3])
    first = iota((COLS, 128), 1) < HALF
    return lane_sum(jnp.where(first, total, 0.0)), lane_sum(jnp.where(first, 0.0, total))


def prolong(base, aggs, values):
    for k in range(COLS):
        value = jnp.concatenate([v[k : k + 1] for v in values], axis=0)
        base = base + jnp.where(aggs == float(k), value, 0.0)
    return base


def sweep(z_win, tiles, rows_ref, sum_ref):
    src, k_ref, sem = tiles
    rows_ref[...] = stacked(z_win)

    def one(i, carry):
        pltpu.make_async_copy(src.at[i], k_ref.at[i], sem.at[i]).wait()
        at = pl.multiple_of(i * BLOCK, BLOCK)
        lhs = rows_ref[:, pl.ds(at, SPAN * BLOCK)]
        acc = jnp.dot(lhs, k_ref[i, 0], preferred_element_type=F32)
        acc = acc + jnp.dot(lhs, k_ref[i, 1], preferred_element_type=F32)
        sum_ref[:, pl.ds(at, BLOCK)] = fold(acc)
        return carry

    lax.fori_loop(0, OWN, one, 0)
    return SHIFT * z_win[:, MID] + KERNEL_SCALE * sum_ref[...]


def start_tiles(tiles):
    src, k_ref, sem = tiles
    for i in range(OWN):
        pltpu.make_async_copy(src.at[i], k_ref.at[i], sem.at[i]).start()


def setup_kernel(subs, me, ins, outs, wide):
    res, agg, coarse, coords, noise = ins
    pay, mine, fine = outs
    device = me[0]
    last = pay.ref.shape[1] - 8
    lane_base = 2 * (device % (CORES * subs))
    r = res()[...]
    agg_line = agg()[...].astype(F32)
    near = agg_line - (2 * device - 1).astype(F32)
    line = payload_line(lane_base, restrict(r, near), [])
    rows, centres = coarse.ref.shape
    first_col = device // (CORES * subs) * (2 * CORES * subs) - 4
    first_row = device % subs * rows
    c = coarse()[...]
    sel = (iota((WIDE, centres), 1) == first_col + iota((WIDE, centres), 0)).astype(BF16)
    c_sel = lax.dot_general(sel, c, (((1,), (1,)), ((), ())), preferred_element_type=F32)
    e_sel = (first_row + iota((WIDE, rows), 1) == first_col + iota((WIDE, rows), 0)).astype(F32)
    both = jnp.concatenate([c_sel, e_sel], axis=0).astype(BF16)
    full = jnp.dot(both, c, preferred_element_type=F32)
    full = full[:WIDE] + full[WIDE:]
    extra = c_sel + e_sel
    if wide.shape[1] > centres:
        wide[...] = jnp.zeros_like(wide)
    wide[:, 0:centres] = full
    start = pl.multiple_of(first_row, rows)
    wide[:, pl.ds(start, rows)] = wide[:, pl.ds(start, rows)] + extra
    for slot in range(CORES * subs):
        low = 2 * slot + 1
        for v in range(last // 8):
            piece = wide[low : low + COLS, v * 128 : (v + 1) * 128]
            pay.ref[slot, v * 8 : v * 8 + 8] = piece
        pay.ref[slot, last : last + 8] = jnp.broadcast_to(line, (8, 128))
    for b in range(OWN):
        n = noise.ref[b]
        nt = n.T
        f = jnp.dot(nt, n, precision=HIGHEST, preferred_element_type=F32) + (n + nt)
        fine.ref[b, 0], fine.ref[b, 1] = split2(f)
    mine.ref[0:3] = coords()[...]
    mine.ref[3:4] = agg_line
    mine.ref[4:6] = fine_apply(r, fine.ref)
    mine.ref[6:8] = jnp.zeros((2, POINTS), F32)


def tile_kernel(
    subs, me, pairs, live_count, ins, outs, k_out, k_ref, xyz, tall, present, k_sem
):
    near_a, near_b, parts, own = ins
    aggs, zb, g_lines = outs
    device = me[0]

    def clear(t, carry):
        present[t] = 0
        return carry

    def mark(s, carry):
        row, col = pairs[0, s], pairs[1, s]
        present[(row - device * OWN) * SPAN + (col - row + REACH)] = 1
        return carry

    lax.fori_loop(0, OWN * SPAN, clear, 0)
    lax.fori_loop(0, live_count[0], mark, 0)
    odd = device % 2 == 1
    a, b = near_a()[...], near_b()[...]
    xyz[:, 0:POINTS] = jnp.where(odd, a, b)
    xyz[:, MID] = own()[...]
    xyz[:, 2 * POINTS : WIN] = jnp.where(odd, b, a)
    aggs.put(xyz[3:4] - (2 * device - 3).astype(F32))
    zb.put(xyz[4:6])

    def one(t, carry):
        i = t // SPAN
        o = t - i * SPAN
        live = present[t]
        spot = pl.ds(pl.multiple_of(o * BLOCK, BLOCK), BLOCK)

        @pl.when(live > 0)
        def _():
            row = xyz[:, pl.ds(pl.multiple_of((i + REACH) * BLOCK, BLOCK), BLOCK)]
            col = xyz[:, pl.ds(pl.multiple_of((i + o) * BLOCK, BLOCK), BLOCK)].T
            d2 = (col[:, 0:1] - row[0:1]) ** 2
            d2 = d2 + (col[:, 1:2] - row[1:2]) ** 2
            d2 = d2 + (col[:, 2:3] - row[2:3]) ** 2
            dist = d2 * lax.rsqrt(jnp.maximum(d2, 1e-30))
            fall = jnp.maximum(1.0 - dist, 0.0)
            fall = fall * fall
            hi, lo = split2((fall * fall) * (4.0 * dist + 1.0))
            k_ref[i, 0, spot] = hi
            k_ref[i, 1, spot] = lo

        @pl.when(live == 0)
        def _():
            zero = jnp.zeros((BLOCK, BLOCK), BF16)
            k_ref[i, 0, spot] = zero
            k_ref[i, 1, spot] = zero

        @pl.when(o == SPAN - 1)
        def _():
            pltpu.make_async_copy(k_ref.at[i], k_out.at[i], k_sem.at[i]).start()

        return carry

    lax.fori_loop(0, OWN * SPAN, one, 0)
    zero = jnp.zeros((COLS, 128), F32)
    span = tall.shape[1] - 256
    tall[:, 0:128] = zero
    for v in range(span // 128):
        total = parts.ref[0, v * 8 : v * 8 + 8]
        for s in range(1, subs):
            total = total + parts.ref[s, v * 8 : v * 8 + 8]
        tall[:, 128 + v * 128 : 256 + v * 128] = total * (AGG ** (-0.5))
    tall[:, 128 + span :] = zero
    lane = iota((COLS, 128), 1)
    step = 2 * CORES * subs
    count = step + 2
    for g in range(g_lines.ref.shape[1] // 128):
        at = 128 + step * g - 1
        lo, off = at // 128 * 128, at % 128
        line = tall[:, lo : lo + 128]
        if off:
            line = pltpu.roll(line, 128 - off, 1)
        if off + count > 128:
            after = pltpu.roll(tall[:, lo + 128 : lo + 256], 128 - off, 1)
            line = jnp.where(lane < 128 - off, line, after)
        line = jnp.where(lane < count, line, 0.0)
        g_lines.ref[:, g * 128 : (g + 1) * 128] = line + pltpu.roll(line, HALF, 1)
    for i in range(OWN):
        pltpu.make_async_copy(k_ref.at[i], k_out.at[i], k_sem.at[i]).wait()


def first_kernel(subs, me, ins, outs, k_src, k_ref, rows_ref, sum_ref, k_sem):
    gath, g_lines, zb, aggs, res, fine = ins
    z_out, w_out, pay, mw_out, cr_out = outs
    tiles = (k_src, k_ref, k_sem)
    start_tiles(tiles)
    device = me[0]
    cr_out.put(gath()[...])
    g_lines()
    z_win = prolong(zb()[...], aggs()[...], coarse_values(gath.ref, g_lines.ref))
    z = z_win[:, MID]
    z_out.put(z)
    w = sweep(z_win, tiles, rows_ref, sum_ref)
    w_out.put(w)
    mw_out.put(fine_apply(w, fine()))
    near = aggs.ref[:, MID] - 2.0
    dots = [lane_sum(res()[...] * z), lane_sum(z * w)]
    payload(pay, 2 * (device % (CORES * subs)), restrict(w, near), dots)


def step_kernel(subs, first, last, extra, me, ins, outs, *raw):
    ins, outs = list(ins), list(outs)
    device = me[0]
    take = lambda k: [ins.pop(0) for _ in range(k)]
    give = lambda k: [outs.pop(0) for _ in range(k)]
    (gath,) = take(1)
    near_mw = [] if last else take(2)
    z, w, x, r, cr, mw_o, zb, aggs, g_lines = take(9)
    d_old = q_old = crq_old = mq_old = rz_old = curve_old = None
    if not first:
        rz_old, curve_old, d_old, q_old, crq_old, mq_old = take(6)
    if last:
        (coarse,) = take(1)
        (vec_ref,) = raw
        x_out, r_out, d_out, z_out, rz_out, fine_out, cr_out, pay = give(8)
    else:
        x_out, r_out, d_out, q_out, rz_out, curve_out, crq_out, mq_out = give(8)
        cr_out, zb_out, z_out, w_out, mw_out, pay = give(6)
        (fine,) = take(1)
        k_src, k_ref, rows_ref, sum_ref, k_sem = raw
        tiles = (k_src, k_ref, k_sem)
        start_tiles(tiles)

    got = gath()[...]
    total = jnp.sum(got, axis=0, keepdims=True)
    rz, zw = pick(total, 0), pick(total, 1)
    mw = mw_o()[...]
    if not last:
        odd = device % 2 == 1
        a, b = [item()[...] for item in near_mw]
        mw = jnp.concatenate([jnp.where(odd, a, b), mw, jnp.where(odd, b, a)], axis=1)
    if first:
        curve = zw
        d, q, crq, mq = z()[...], w()[...], got, mw
    else:
        beta = rz / rz_old()[:, 0:1]
        curve = zw + beta * (2.0 * pick(total, 2) + beta * curve_old()[:, 0:1])
        d = z()[...] + beta * d_old()[...]
        q = w()[...] + beta * q_old()[...]
        crq = got + spread(beta) * crq_old()[...]
        mq = mw + beta * (mq_old()[:, MID] if last else mq_old()[...])
    alpha = rz / curve
    r_new = r()[...] - alpha * q
    x_out.put(alpha * d if first else x()[...] + alpha * d)
    r_out.put(r_new)
    d_out.put(d)
    rz_out.put(jnp.broadcast_to(rz, rz_out.ref.shape))
    cr_new = cr()[...] - spread(alpha) * crq
    zb_new = (zb()[:, MID] if last else zb()[...]) - alpha * mq
    cr_out.put(cr_new)
    values = coarse_values(cr_out.ref, g_lines())
    if last:
        z_new = prolong(zb_new, aggs()[:, MID], values)
        z_out.put(z_new)
        e = [pick(total, 3 + i) for i in range(6)]
        linear = e[1] + beta * e[2]
        square = e[3] + beta * (2.0 * e[4] + beta * e[5])
        fine = e[0] + alpha * (alpha * square - 2.0 * linear)
        fine_out.put(jnp.broadcast_to(fine, fine_out.ref.shape))
        lay_out(cr_out.ref, vec_ref, 2 * CORES * subs)
        rows, centres = coarse.ref.shape
        lhs = stacked(vec_ref[:, 128 : 128 + centres])
        y = fold(
            lax.dot_general(
                lhs, coarse()[...], (((1,), (1,)), ((), ())), preferred_element_type=F32
            )
        )
        start = pl.multiple_of(device % subs * rows, rows)
        y = y + vec_ref[:, pl.ds(128 + start, rows)]
        payload(pay, 0, [], [lane_sum(y * y) * (AGG ** (-0.5))])
        return
    zb_out.put(zb_new)
    q_out.put(q)
    crq_out.put(crq)
    mq_out.put(mq)
    curve_out.put(jnp.broadcast_to(curve, curve_out.ref.shape))
    z_win = prolong(zb_new, aggs()[...], values)
    z_new = z_win[:, MID]
    z_out.put(z_new)
    w_new = sweep(z_win, tiles, rows_ref, sum_ref)
    w_out.put(w_new)
    mw_out.put(fine_apply(w_new, fine()))
    dots = [lane_sum(r_new * z_new), lane_sum(z_new * w_new), lane_sum(z_new * q)]
    if extra:
        zb_mid, mw_new, mq_mid = zb_new[:, MID], mw_out.ref[...], mq[:, MID]
        pairs = [(r_new, zb_mid), (w_new, zb_mid), (q, zb_mid)]
        pairs = pairs + [(w_new, mw_new), (w_new, mq_mid), (q, mq_mid)]
        dots = dots + [lane_sum(a * b) for a, b in pairs]
    near = aggs.ref[:, MID] - 2.0
    payload(pay, 2 * (device % (CORES * subs)), restrict(w_new, near), dots)


def lay_out(cr_ref, vec_ref, step):
    lane = iota((1, 128), 1)
    zero = jnp.zeros((1, 128), F32)
    sums = [[zero] * (vec_ref.shape[1] // 128) for _ in range(2)]
    for g in range(cr_ref.shape[0]):
        at = 128 + step * g - 1
        v, off = at // 128, at % 128
        line = cr_ref[g : g + 1, :]
        end = off + step + 2
        for f in range(2):
            moved = pltpu.roll(line, (off + f * HALF) % 128, 1)
            here = (lane >= off) & (lane < end)
            sums[f][v] = sums[f][v] + jnp.where(here, moved, 0.0)
            if end > 128:
                sums[f][v + 1] = sums[f][v + 1] + jnp.where(lane < end - 128, moved, 0.0)
    for v in range(len(sums[0])):
        both = jnp.concatenate([sums[0][v], sums[1][v]], axis=0)
        vec_ref[:, v * 128 : (v + 1) * 128] = both


def last_kernel(ins, outs):
    coarse, z, d_old, rz_old, fine = ins
    (d_out,) = outs
    total = jnp.sum(coarse()[...], axis=0, keepdims=True)
    beta = (pick(total, 0) + fine()[:, 0:1]) / rz_old()[:, 0:1]
    d_out.put(z()[...] + beta * d_old()[...])


def neighbours(block):
    count = lax.axis_size(AXES)
    inner = [(i, i ^ 1) for i in range(count)]
    outer = [(i, i + 1) for i in range(1, count - 1, 2)]
    outer = outer + [(i + 1, i) for i in range(1, count - 1, 2)]
    return lax.ppermute(block, AXES, inner), lax.ppermute(block, AXES, outer)


def first_stage(rows):
    return lax.all_to_all(rows, ("core", "sub"), 0, 0, tiled=True)


def second_stage(near):
    groups = lax.axis_size("grp")
    total = jnp.broadcast_to(jnp.sum(near, axis=0, keepdims=True), (groups, 128))
    return lax.all_to_all(total, "grp", 0, 0, tiled=True)


def per_device(coords, right_side, tile_pairs, tile_count, fine_noise, coarse_noise, aggregate):
    fields = right_side.shape[0]
    subs, groups = lax.axis_size("sub"), lax.axis_size("grp")
    centres = coarse_noise.shape[1]
    device = (lax.axis_index("grp") * CORES + lax.axis_index("core")) * subs
    me = jnp.full((1,), device + lax.axis_index("sub"), jnp.int32)
    vec, win = ((fields, POINTS), F32), ((fields, WIN), F32)
    line, small = ((groups, 128), F32), ((fields, 128), F32)
    row = ((CORES * subs, 128), F32)
    tiles = ((OWN, 2, SPAN * BLOCK, BLOCK), BF16)
    fines = ((OWN, 2, BLOCK, BLOCK), BF16)
    lines = ((COLS, groups * 128), F32)
    sweeping = [
        pltpu.VMEM(*tiles),
        pltpu.VMEM((3 * fields, WIN), BF16),
        pltpu.VMEM(*vec),
        pltpu.SemaphoreType.DMA((OWN,)),
    ]

    span = max(centres, 128)
    pay, mine, fine = call(
        functools.partial(setup_kernel, subs),
        [((CORES * subs, span // 16 + 8, 128), F32), ((8, POINTS), F32), fines],
        scratch=[pltpu.VMEM((WIDE, span), F32)],
        smem=1,
    )(me, right_side, aggregate[None], coarse_noise, coords, fine_noise)
    near_a, near_b = neighbours(mine)
    parts = first_stage(pay)
    got = second_stage(parts[:, span // 16])
    aggs, zb, g_lines, kernel_tiles = call(
        functools.partial(tile_kernel, subs),
        [((1, WIN), F32), win, lines],
        raw_outs=[tiles],
        scratch=[
            pltpu.VMEM(*tiles),
            pltpu.VMEM((8, WIN), F32),
            pltpu.VMEM((COLS, span + 256), F32),
            pltpu.SMEM((OWN * SPAN,), jnp.int32),
            pltpu.SemaphoreType.DMA((OWN,)),
        ],
        smem=3,
    )(me, tile_pairs, tile_count, near_a, near_b, parts, mine)

    z, w, pay, mw, cr = call(
        functools.partial(first_kernel, subs),
        [vec, vec, row, vec, line],
        raw=[kernel_tiles],
        scratch=sweeping,
        smem=1,
    )(me, got, g_lines, zb, aggs, right_side, fine)
    x, r = right_side, right_side
    old = ()
    for iteration in range(ITERS):
        first, last = iteration == 0, iteration == ITERS - 1
        got = second_stage(first_stage(pay))
        state = (z, w, x, r, cr, mw, zb, aggs, g_lines)
        body = functools.partial(step_kernel, subs, first, last, iteration == ITERS - 2)
        if last:
            outs = [vec, vec, vec, vec, small, small, line, ((subs, 128), F32)]
            room = [pltpu.VMEM((fields, span + 256), F32)]
            run = call(body, outs, scratch=room, smem=1)
            x, r, d, z, rz, fine_rz, _, pay = run(me, got, *state, *old, coarse_noise)
        else:
            outs = [vec] * 4 + [small, small, line, win, line, win, vec, vec, vec, row]
            run = call(body, outs, raw=[kernel_tiles], scratch=sweeping, smem=1)
            x, r, d, q, rz, curve, crq, mq, cr, zb, z, w, mw, pay = run(
                me, got, *neighbours(mw), *state, *old, fine
            )
            old = (rz, curve, d, q, crq, mq)
    coarse_rz = lax.all_to_all(pay, "sub", 0, 0, tiled=True)
    (d,) = call(last_kernel, [vec])(coarse_rz, z, d, rz, fine_rz)
    return (x, r, d)


def solution(mesh):
    devices = mesh.devices
    blk, subs = devices.shape
    fine_mesh = Mesh(devices.reshape(blk // CORES, CORES, subs), AXES)
    points = P(None, AXES)
    in_specs = (
        points,
        points,
        points,
        P(AXES),
        P(AXES, None, None),
        P("sub", None),
        P(AXES),
    )
    return jax.shard_map(
        per_device, mesh=fine_mesh, in_specs=in_specs, out_specs=(points,) * 3, check_vma=False
    )
```

```python
import functools

import jax
import jax.numpy as jnp
from jax import lax
from jax.experimental import pallas as pl
from jax.experimental.pallas import tpu as pltpu
from jax.sharding import Mesh
from jax.sharding import PartitionSpec as P

BLOCK = 256
REACH = 4
AGG = 512
ITERS = 4
SHIFT = 1.5
KERNEL_SCALE = 1.0 / (BLOCK * (2 * REACH + 1))
OWN = 4
POINTS = OWN * BLOCK
WIN = 3 * POINTS
MID = slice(POINTS, 2 * POINTS)
SPAN = 2 * REACH + 1
HALF = 64
DOTS = 32
NEAR = 4
COLS = 8
WIDE = 32
CORES = 2
STRIP = 16
AXES = ("grp", "core", "sub")
VMEM_LIMIT = 48 * 1024 * 1024
SETUP_LIMIT = 56 * 1024 * 1024
F32 = jnp.float32
BF16 = jnp.bfloat16
HIGHEST = lax.Precision.HIGHEST


class Operand:
    def __init__(self, ref):
        self.ref = ref

    def __call__(self):
        return self.ref

    def put(self, value):
        self.ref[...] = value


def call(body, outs, raw=(), raw_outs=(), scratch=(), smem=0, limit=None):
    def run(*args):
        n, m = len(args) - smem, len(outs)
        p, q = len(raw), len(raw_outs)

        def kernel(*refs):
            refs = list(refs)
            take = lambda k: [refs.pop(0) for _ in range(k)]
            scalars, ins, raw_in = take(smem), take(n), take(p)
            results, raw_out = take(m), take(q)
            body(
                *scalars,
                [Operand(ref) for ref in ins],
                [Operand(ref) for ref in results],
                *raw_in,
                *raw_out,
                *refs,
            )

        smem_spec = pl.BlockSpec(memory_space=pltpu.SMEM)
        vmem_spec = pl.BlockSpec(memory_space=pltpu.VMEM)
        hbm_spec = pl.BlockSpec(memory_space=pltpu.HBM)
        return pl.pallas_call(
            kernel,
            out_shape=[jax.ShapeDtypeStruct(s, d) for s, d in list(outs) + list(raw_outs)],
            in_specs=[smem_spec] * smem + [vmem_spec] * n + [hbm_spec] * p,
            out_specs=[vmem_spec] * m + [hbm_spec] * q,
            scratch_shapes=list(scratch),
            compiler_params=pltpu.CompilerParams(vmem_limit_bytes=limit or VMEM_LIMIT),
        )(*args, *raw)

    return run


def iota(shape, dim):
    return lax.broadcasted_iota(jnp.int32, shape, dim)


def split2(x):
    hi = x.astype(BF16)
    return hi, (x - hi.astype(F32)).astype(BF16)


def stacked(x):
    hi = x.astype(BF16).astype(F32)
    rest = x - hi
    mid = rest.astype(BF16).astype(F32)
    return jnp.concatenate([hi, mid, rest - mid], axis=0).astype(BF16)


def fold(acc):
    return acc[0:2] + acc[2:4] + acc[4:6]


def lane_sum(x):
    return jnp.sum(x, axis=1, keepdims=True)


def fine_apply(vec, fine):
    rows = stacked(vec)
    parts = []
    for b in range(OWN):
        lhs = rows[:, b * BLOCK : (b + 1) * BLOCK]
        acc = jnp.dot(lhs, fine[b, 0], preferred_element_type=F32)
        acc = acc + jnp.dot(lhs, fine[b, 1], preferred_element_type=F32)
        parts.append(fold(acc))
    return vec + jnp.concatenate(parts, axis=1)


def payload_line(base, coarse, dots):
    lane, row = iota((2, 128), 1), iota((2, 128), 0)
    tile = jnp.zeros((2, 128), F32)
    for slot, value in enumerate(coarse):
        tile = jnp.where(lane == row * HALF + base + slot, value, tile)
    for slot, value in enumerate(dots):
        tile = jnp.where(lane == row * HALF + DOTS + slot, value, tile)
    return jnp.sum(tile, axis=0, keepdims=True)


def payload(out, base, coarse, dots):
    out.put(jnp.broadcast_to(payload_line(base, coarse, dots), out.ref.shape))


def restrict(vec, near):
    return [lane_sum(jnp.where(near == float(k), vec, 0.0)) for k in range(NEAR)]


def group_sums(rows_ref, size):
    rows = rows_ref[...]
    return jnp.sum(rows.reshape(rows.shape[0] // size, size, 128), axis=1)


def pick(line, slot):
    lane, row = iota((2, 128), 1), iota((2, 128), 0)
    return lane_sum(jnp.where(lane == row * HALF + DOTS + slot, line, 0.0))


def spread(value):
    return jnp.where(iota((1, 128), 1) < HALF, value[0:1], value[1:2])


def coarse_values(cr_ref, g_ref):
    acc = [jnp.zeros((COLS, 128), F32) for _ in range(4)]
    for g in range(cr_ref.shape[0]):
        acc[g % 4] = acc[g % 4] + g_ref[:, g * 128 : (g + 1) * 128] * cr_ref[g : g + 1, :]
    total = (acc[0] + acc[1]) + (acc[2] + acc[3])
    first = iota((COLS, 128), 1) < HALF
    return lane_sum(jnp.where(first, total, 0.0)), lane_sum(jnp.where(first, 0.0, total))


def prolong(base, aggs, values):
    for k in range(COLS):
        value = jnp.concatenate([v[k : k + 1] for v in values], axis=0)
        base = base + jnp.where(aggs == float(k), value, 0.0)
    return base


def sweep(z_win, tiles, rows_ref, sum_ref):
    src, k_ref, sem = tiles
    rows_ref[...] = stacked(z_win)

    def one(i, carry):
        pltpu.make_async_copy(src.at[i], k_ref.at[i], sem.at[i]).wait()
        at = pl.multiple_of(i * BLOCK, BLOCK)
        lhs = rows_ref[:, pl.ds(at, SPAN * BLOCK)]
        acc = jnp.dot(lhs, k_ref[i, 0], preferred_element_type=F32)
        acc = acc + jnp.dot(lhs, k_ref[i, 1], preferred_element_type=F32)
        sum_ref[:, pl.ds(at, BLOCK)] = fold(acc)
        return carry

    lax.fori_loop(0, OWN, one, 0)
    return SHIFT * z_win[:, MID] + KERNEL_SCALE * sum_ref[...]


def start_tiles(tiles):
    src, k_ref, sem = tiles
    for i in range(OWN):
        pltpu.make_async_copy(src.at[i], k_ref.at[i], sem.at[i]).start()


def setup_kernel(subs, me, ins, outs, *raw):
    sources, held = raw[:5], raw[5:10]
    wide, sem = raw[10:]
    copies = [
        pltpu.make_async_copy(source, ref, sem.at[i])
        for i, (source, ref) in enumerate(zip(sources, held))
    ]
    for copy in copies:
        copy.start()
    res, agg, coarse, coords, noise = [Operand(ref) for ref in held]
    pay, mine, fine, res_out = outs
    for copy in copies[:3]:
        copy.wait()
    res_out.put(res()[...])
    device = me[0]
    last = pay.ref.shape[1] - 8
    lane_base = 2 * (device % (CORES * subs))
    r = res()[...]
    agg_line = agg()[...].astype(F32)
    near = agg_line - (2 * device - 1).astype(F32)
    line = payload_line(lane_base, restrict(r, near), [])
    rows, centres = coarse.ref.shape
    first_col = device // (CORES * subs) * (2 * CORES * subs) - 4
    first_row = device % subs * rows
    c = coarse()[...]
    sel = (iota((WIDE, centres), 1) == first_col + iota((WIDE, centres), 0)).astype(BF16)
    c_sel = lax.dot_general(sel, c, (((1,), (1,)), ((), ())), preferred_element_type=F32)
    e_sel = (first_row + iota((WIDE, rows), 1) == first_col + iota((WIDE, rows), 0)).astype(F32)
    both = jnp.concatenate([c_sel, e_sel], axis=0).astype(BF16)
    full = jnp.dot(both, c, preferred_element_type=F32)
    full = full[:WIDE] + full[WIDE:]
    extra = c_sel + e_sel
    if wide.shape[1] > centres:
        wide[...] = jnp.zeros_like(wide)
    wide[:, 0:centres] = full
    start = pl.multiple_of(first_row, rows)
    wide[:, pl.ds(start, rows)] = wide[:, pl.ds(start, rows)] + extra
    for slot in range(CORES * subs):
        low = 2 * slot + 1
        for v in range(last // 8):
            piece = wide[low : low + COLS, v * 128 : (v + 1) * 128]
            pay.ref[slot, v * 8 : v * 8 + 8] = piece
        pay.ref[slot, last : last + 8] = jnp.broadcast_to(line, (8, 128))
    for copy in copies[3:]:
        copy.wait()
    for b in range(OWN):
        n = noise.ref[b]
        nt = n.T
        f = jnp.dot(nt, n, precision=HIGHEST, preferred_element_type=F32) + (n + nt)
        fine.ref[b, 0], fine.ref[b, 1] = split2(f)
    mine.ref[0:3] = coords()[...]
    mine.ref[3:4] = agg_line
    mine.ref[4:6] = fine_apply(r, fine.ref)
    mine.ref[6:8] = jnp.zeros((2, POINTS), F32)


def tile_kernel(
    subs, me, pairs, live_count, ins, outs, k_out, k_ref, xyz, tall_xyz, tall, present, k_sem
):
    near_a, near_b, parts, own = ins
    aggs, zb, g_lines = outs
    device = me[0]

    def clear(t, carry):
        present[t] = 0
        return carry

    def mark(s, carry):
        row, col = pairs[0, s], pairs[1, s]
        present[(row - device * OWN) * SPAN + (col - row + REACH)] = 1
        return carry

    lax.fori_loop(0, OWN * SPAN, clear, 0)
    lax.fori_loop(0, live_count[0], mark, 0)
    odd = device % 2 == 1
    a, b = near_a()[...], near_b()[...]
    xyz[:, 0:POINTS] = jnp.where(odd, a, b)
    xyz[:, MID] = own()[...]
    xyz[:, 2 * POINTS : WIN] = jnp.where(odd, b, a)
    aggs.put(xyz[3:4] - (2 * device - 3).astype(F32))
    zb.put(xyz[4:6])

    for j in range(WIN // BLOCK):
        tall_xyz[j * BLOCK : (j + 1) * BLOCK, 0:8] = xyz[:, j * BLOCK : (j + 1) * BLOCK].T

    def one(t, carry):
        i = t // SPAN
        o = t - i * SPAN
        live = present[t]
        spot = pl.ds(pl.multiple_of(o * BLOCK, BLOCK), BLOCK)

        @pl.when(live > 0)
        def _():
            row = xyz[0:3, pl.ds(pl.multiple_of((i + REACH) * BLOCK, BLOCK), BLOCK)]
            rows = [jnp.broadcast_to(row[c : c + 1], (STRIP, BLOCK)) for c in range(3)]

            def strip(s, carry):
                at = pl.multiple_of((i + o) * BLOCK + s * STRIP, STRIP)
                col = tall_xyz[pl.ds(at, STRIP), 0:8]
                d2 = (col[:, 0:1] - rows[0]) ** 2
                d2 = d2 + (col[:, 1:2] - rows[1]) ** 2
                d2 = d2 + (col[:, 2:3] - rows[2]) ** 2
                dist = d2 * lax.rsqrt(jnp.maximum(d2, 1e-30))
                fall = jnp.maximum(1.0 - dist, 0.0)
                fall = fall * fall
                hi, lo = split2((fall * fall) * (4.0 * dist + 1.0))
                to = pl.ds(pl.multiple_of(o * BLOCK + s * STRIP, STRIP), STRIP)
                k_ref[i, 0, to] = hi
                k_ref[i, 1, to] = lo
                return carry

            lax.fori_loop(0, BLOCK // STRIP, strip, 0, unroll=8)

        @pl.when(live == 0)
        def _():
            zero = jnp.zeros((BLOCK, BLOCK), BF16)
            k_ref[i, 0, spot] = zero
            k_ref[i, 1, spot] = zero

        @pl.when(o == SPAN - 1)
        def _():
            pltpu.make_async_copy(k_ref.at[i], k_out.at[i], k_sem.at[i]).start()

        return carry

    lax.fori_loop(0, OWN * SPAN, one, 0)
    zero = jnp.zeros((COLS, 128), F32)
    span = tall.shape[1] - 256
    tall[:, 0:128] = zero
    for v in range(span // 128):
        total = parts.ref[0, v * 8 : v * 8 + 8]
        for s in range(1, subs):
            total = total + parts.ref[s, v * 8 : v * 8 + 8]
        tall[:, 128 + v * 128 : 256 + v * 128] = total * (AGG ** (-0.5))
    tall[:, 128 + span :] = zero
    lane = iota((COLS, 128), 1)
    step = 2 * CORES * subs
    count = step + 2
    for g in range(g_lines.ref.shape[1] // 128):
        at = 128 + step * g - 1
        lo, off = at // 128 * 128, at % 128
        line = tall[:, lo : lo + 128]
        if off:
            line = pltpu.roll(line, 128 - off, 1)
        if off + count > 128:
            after = pltpu.roll(tall[:, lo + 128 : lo + 256], 128 - off, 1)
            line = jnp.where(lane < 128 - off, line, after)
        line = jnp.where(lane < count, line, 0.0)
        g_lines.ref[:, g * 128 : (g + 1) * 128] = line + pltpu.roll(line, HALF, 1)
    for i in range(OWN):
        pltpu.make_async_copy(k_ref.at[i], k_out.at[i], k_sem.at[i]).wait()


def first_kernel(subs, me, ins, outs, k_src, k_ref, rows_ref, sum_ref, k_sem):
    gath, g_lines, zb, aggs, res, fine = ins
    z_out, w_out, pay, mw_out, cr_out = outs
    tiles = (k_src, k_ref, k_sem)
    start_tiles(tiles)
    device = me[0]
    cr_out.put(gath()[...])
    g_lines()
    z_win = prolong(zb()[...], aggs()[...], coarse_values(gath.ref, g_lines.ref))
    z = z_win[:, MID]
    z_out.put(z)
    w = sweep(z_win, tiles, rows_ref, sum_ref)
    w_out.put(w)
    mw_out.put(fine_apply(w, fine()))
    near = aggs.ref[:, MID] - 2.0
    dots = [lane_sum(res()[...] * z), lane_sum(z * w)]
    payload(pay, 2 * (device % (CORES * subs)), restrict(w, near), dots)


def step_kernel(subs, first, last, extra, me, ins, outs, *raw):
    ins, outs = list(ins), list(outs)
    device = me[0]
    take = lambda k: [ins.pop(0) for _ in range(k)]
    give = lambda k: [outs.pop(0) for _ in range(k)]
    (gath,) = take(1)
    near_mw = [] if last else take(2)
    z, w, x, r, cr, mw_o, zb, aggs, g_lines = take(9)
    d_old = q_old = crq_old = mq_old = rz_old = curve_old = None
    if not first:
        rz_old, curve_old, d_old, q_old, crq_old, mq_old = take(6)
    if last:
        (coarse,) = take(1)
        (vec_ref,) = raw
        x_out, r_out, d_out, z_out, rz_out, fine_out, cr_out, pay = give(8)
    else:
        x_out, r_out, d_out, q_out, rz_out, curve_out, crq_out, mq_out = give(8)
        cr_out, zb_out, z_out, w_out, mw_out, pay = give(6)
        (fine,) = take(1)
        k_src, k_ref, rows_ref, sum_ref, k_sem = raw
        tiles = (k_src, k_ref, k_sem)
        start_tiles(tiles)

    got = group_sums(gath.ref, CORES * subs)
    total = jnp.sum(got, axis=0, keepdims=True)
    rz, zw = pick(total, 0), pick(total, 1)
    mw = mw_o()[...]
    if not last:
        odd = device % 2 == 1
        a, b = [item()[...] for item in near_mw]
        mw = jnp.concatenate([jnp.where(odd, a, b), mw, jnp.where(odd, b, a)], axis=1)
    if first:
        curve = zw
        d, q, crq, mq = z()[...], w()[...], got, mw
    else:
        beta = rz / rz_old()[:, 0:1]
        curve = zw + beta * (2.0 * pick(total, 2) + beta * curve_old()[:, 0:1])
        d = z()[...] + beta * d_old()[...]
        q = w()[...] + beta * q_old()[...]
        crq = got + spread(beta) * crq_old()[...]
        mq = mw + beta * (mq_old()[:, MID] if last else mq_old()[...])
    alpha = rz / curve
    r_new = r()[...] - alpha * q
    x_out.put(alpha * d if first else x()[...] + alpha * d)
    r_out.put(r_new)
    d_out.put(d)
    rz_out.put(jnp.broadcast_to(rz, rz_out.ref.shape))
    cr_new = cr()[...] - spread(alpha) * crq
    zb_new = (zb()[:, MID] if last else zb()[...]) - alpha * mq
    cr_out.put(cr_new)
    values = coarse_values(cr_out.ref, g_lines())
    if last:
        z_new = prolong(zb_new, aggs()[:, MID], values)
        z_out.put(z_new)
        e = [pick(total, 3 + i) for i in range(6)]
        linear = e[1] + beta * e[2]
        square = e[3] + beta * (2.0 * e[4] + beta * e[5])
        fine = e[0] + alpha * (alpha * square - 2.0 * linear)
        fine_out.put(jnp.broadcast_to(fine, fine_out.ref.shape))
        lay_out(cr_out.ref, vec_ref, 2 * CORES * subs)
        rows, centres = coarse.ref.shape
        lhs = stacked(vec_ref[:, 128 : 128 + centres])
        y = fold(
            lax.dot_general(
                lhs, coarse()[...], (((1,), (1,)), ((), ())), preferred_element_type=F32
            )
        )
        start = pl.multiple_of(device % subs * rows, rows)
        y = y + vec_ref[:, pl.ds(128 + start, rows)]
        payload(pay, 0, [], [lane_sum(y * y) * (AGG ** (-0.5))])
        return
    zb_out.put(zb_new)
    q_out.put(q)
    crq_out.put(crq)
    mq_out.put(mq)
    curve_out.put(jnp.broadcast_to(curve, curve_out.ref.shape))
    z_win = prolong(zb_new, aggs()[...], values)
    z_new = z_win[:, MID]
    z_out.put(z_new)
    w_new = sweep(z_win, tiles, rows_ref, sum_ref)
    w_out.put(w_new)
    mw_out.put(fine_apply(w_new, fine()))
    dots = [lane_sum(r_new * z_new), lane_sum(z_new * w_new), lane_sum(z_new * q)]
    if extra:
        zb_mid, mw_new, mq_mid = zb_new[:, MID], mw_out.ref[...], mq[:, MID]
        pairs = [(r_new, zb_mid), (w_new, zb_mid), (q, zb_mid)]
        pairs = pairs + [(w_new, mw_new), (w_new, mq_mid), (q, mq_mid)]
        dots = dots + [lane_sum(a * b) for a, b in pairs]
    near = aggs.ref[:, MID] - 2.0
    payload(pay, 2 * (device % (CORES * subs)), restrict(w_new, near), dots)


def lay_out(cr_ref, vec_ref, step):
    lane = iota((1, 128), 1)
    zero = jnp.zeros((1, 128), F32)
    sums = [[zero] * (vec_ref.shape[1] // 128) for _ in range(2)]
    for g in range(cr_ref.shape[0]):
        at = 128 + step * g - 1
        v, off = at // 128, at % 128
        line = cr_ref[g : g + 1, :]
        end = off + step + 2
        for f in range(2):
            moved = pltpu.roll(line, (off + f * HALF) % 128, 1)
            here = (lane >= off) & (lane < end)
            sums[f][v] = sums[f][v] + jnp.where(here, moved, 0.0)
            if end > 128:
                sums[f][v + 1] = sums[f][v + 1] + jnp.where(lane < end - 128, moved, 0.0)
    for v in range(len(sums[0])):
        both = jnp.concatenate([sums[0][v], sums[1][v]], axis=0)
        vec_ref[:, v * 128 : (v + 1) * 128] = both


def last_kernel(ins, outs):
    coarse, z, d_old, rz_old, fine = ins
    (d_out,) = outs
    total = jnp.sum(coarse()[...], axis=0, keepdims=True)
    beta = (pick(total, 0) + fine()[:, 0:1]) / rz_old()[:, 0:1]
    d_out.put(z()[...] + beta * d_old()[...])


def neighbours(block):
    count = lax.axis_size(AXES)
    inner = [(i, i ^ 1) for i in range(count)]
    outer = [(i, i + 1) for i in range(1, count - 1, 2)]
    outer = outer + [(i + 1, i) for i in range(1, count - 1, 2)]
    return lax.ppermute(block, AXES, inner), lax.ppermute(block, AXES, outer)


def first_stage(rows):
    return lax.all_to_all(rows, ("core", "sub"), 0, 0, tiled=True)


def second_stage(near):
    groups = lax.axis_size("grp")
    total = jnp.broadcast_to(jnp.sum(near, axis=0, keepdims=True), (groups, 128))
    return lax.all_to_all(total, "grp", 0, 0, tiled=True)


def per_device(coords, right_side, tile_pairs, tile_count, fine_noise, coarse_noise, aggregate):
    fields = right_side.shape[0]
    subs, groups = lax.axis_size("sub"), lax.axis_size("grp")
    centres = coarse_noise.shape[1]
    device = (lax.axis_index("grp") * CORES + lax.axis_index("core")) * subs
    me = jnp.full((1,), device + lax.axis_index("sub"), jnp.int32)
    vec, win = ((fields, POINTS), F32), ((fields, WIN), F32)
    line, small = ((groups, 128), F32), ((fields, 128), F32)
    row = ((CORES * subs * groups, 128), F32)
    tiles = ((OWN, 2, SPAN * BLOCK, BLOCK), BF16)
    fines = ((OWN, 2, BLOCK, BLOCK), BF16)
    lines = ((COLS, groups * 128), F32)
    sweeping = [
        pltpu.VMEM(*tiles),
        pltpu.VMEM((3 * fields, WIN), BF16),
        pltpu.VMEM(*vec),
        pltpu.SemaphoreType.DMA((OWN,)),
    ]

    span = max(centres, 128)
    params = (right_side, aggregate[None], coarse_noise, coords, fine_noise)
    pay, mine, fine, res = call(
        functools.partial(setup_kernel, subs),
        [((CORES * subs, span // 16 + 8, 128), F32), ((8, POINTS), F32), fines, vec],
        raw=params,
        scratch=[pltpu.VMEM(p.shape, p.dtype) for p in params]
        + [pltpu.VMEM((WIDE, span), F32), pltpu.SemaphoreType.DMA((len(params),))],
        smem=1,
        limit=SETUP_LIMIT,
    )(me)
    near_a, near_b = neighbours(mine)
    parts = first_stage(pay)
    got = second_stage(parts[:, span // 16])
    aggs, zb, g_lines, kernel_tiles = call(
        functools.partial(tile_kernel, subs),
        [((1, WIN), F32), win, lines],
        raw_outs=[tiles],
        scratch=[
            pltpu.VMEM(*tiles),
            pltpu.VMEM((8, WIN), F32),
            pltpu.VMEM((WIN, 8), F32),
            pltpu.VMEM((COLS, span + 256), F32),
            pltpu.SMEM((OWN * SPAN,), jnp.int32),
            pltpu.SemaphoreType.DMA((OWN,)),
        ],
        smem=3,
    )(me, tile_pairs, tile_count, near_a, near_b, parts, mine)

    z, w, pay, mw, cr = call(
        functools.partial(first_kernel, subs),
        [vec, vec, row, vec, line],
        raw=[kernel_tiles],
        scratch=sweeping,
        smem=1,
    )(me, got, g_lines, zb, aggs, res, fine)
    x, r = res, res
    old = ()
    for iteration in range(ITERS):
        first, last = iteration == 0, iteration == ITERS - 1
        got = lax.all_to_all(pay, AXES, 0, 0, tiled=True)
        state = (z, w, x, r, cr, mw, zb, aggs, g_lines)
        body = functools.partial(step_kernel, subs, first, last, iteration == ITERS - 2)
        if last:
            outs = [vec, vec, vec, vec, small, small, line, ((subs, 128), F32)]
            room = [pltpu.VMEM((fields, span + 256), F32)]
            run = call(body, outs, scratch=room, smem=1)
            x, r, d, z, rz, fine_rz, _, pay = run(me, got, *state, *old, coarse_noise)
        else:
            outs = [vec] * 4 + [small, small, line, win, line, win, vec, vec, vec, row]
            run = call(body, outs, raw=[kernel_tiles], scratch=sweeping, smem=1)
            x, r, d, q, rz, curve, crq, mq, cr, zb, z, w, mw, pay = run(
                me, got, *neighbours(mw), *state, *old, fine
            )
            old = (rz, curve, d, q, crq, mq)
    coarse_rz = lax.all_to_all(pay, "sub", 0, 0, tiled=True)
    (d,) = call(last_kernel, [vec])(coarse_rz, z, d, rz, fine_rz)
    return (x, r, d)


def solution(mesh):
    devices = mesh.devices
    blk, subs = devices.shape
    fine_mesh = Mesh(devices.reshape(blk // CORES, CORES, subs), AXES)
    points = P(None, AXES)
    in_specs = (
        points,
        points,
        points,
        P(AXES),
        P(AXES, None, None),
        P("sub", None),
        P(AXES),
    )
    return jax.shard_map(
        per_device, mesh=fine_mesh, in_specs=in_specs, out_specs=(points,) * 3, check_vma=False
    )
```

```python
import functools

import jax
import jax.numpy as jnp
from jax import lax
from jax.experimental import pallas as pl
from jax.experimental.pallas import tpu as pltpu
from jax.sharding import Mesh
from jax.sharding import PartitionSpec as P

BLOCK = 256
REACH = 4
AGG = 512
ITERS = 4
SHIFT = 1.5
KERNEL_SCALE = 1.0 / (BLOCK * (2 * REACH + 1))
OWN = 4
POINTS = OWN * BLOCK
WIN = 3 * POINTS
MID = slice(POINTS, 2 * POINTS)
SPAN = 2 * REACH + 1
HALF = 64
DOTS = 32
NEAR = 4
COLS = 8
WIDE = 32
CORES = 2
STRIP = 16
AXES = ("grp", "core", "sub")
VMEM_LIMIT = 50 * 1024 * 1024
SETUP_LIMIT = 52 * 1024 * 1024
F32 = jnp.float32
BF16 = jnp.bfloat16
HIGHEST = lax.Precision.HIGHEST


class Operand:
    def __init__(self, ref):
        self.ref = ref

    def __call__(self):
        return self.ref

    def put(self, value):
        self.ref[...] = value


def call(body, outs, raw=(), raw_outs=(), scratch=(), smem=0, limit=None):
    def run(*args):
        n, m = len(args) - smem, len(outs)
        p, q = len(raw), len(raw_outs)

        def kernel(*refs):
            refs = list(refs)
            take = lambda k: [refs.pop(0) for _ in range(k)]
            scalars, ins, raw_in = take(smem), take(n), take(p)
            results, raw_out = take(m), take(q)
            body(
                *scalars,
                [Operand(ref) for ref in ins],
                [Operand(ref) for ref in results],
                *raw_in,
                *raw_out,
                *refs,
            )

        smem_spec = pl.BlockSpec(memory_space=pltpu.SMEM)
        vmem_spec = pl.BlockSpec(memory_space=pltpu.VMEM)
        hbm_spec = pl.BlockSpec(memory_space=pltpu.HBM)
        return pl.pallas_call(
            kernel,
            out_shape=[jax.ShapeDtypeStruct(s, d) for s, d in list(outs) + list(raw_outs)],
            in_specs=[smem_spec] * smem + [vmem_spec] * n + [hbm_spec] * p,
            out_specs=[vmem_spec] * m + [hbm_spec] * q,
            scratch_shapes=list(scratch),
            compiler_params=pltpu.CompilerParams(vmem_limit_bytes=limit or VMEM_LIMIT),
        )(*args, *raw)

    return run


def iota(shape, dim):
    return lax.broadcasted_iota(jnp.int32, shape, dim)


def split2(x):
    hi = x.astype(BF16)
    return hi, (x - hi.astype(F32)).astype(BF16)


def stacked(x):
    hi = x.astype(BF16).astype(F32)
    rest = x - hi
    mid = rest.astype(BF16).astype(F32)
    return jnp.concatenate([hi, mid, rest - mid], axis=0).astype(BF16)


def fold(acc):
    return acc[0:2] + acc[2:4] + acc[4:6]


def lane_sum(x):
    return jnp.sum(x, axis=1, keepdims=True)


def fine_apply(vec, fine):
    rows = stacked(vec)
    parts = []
    for b in range(OWN):
        lhs = rows[:, b * BLOCK : (b + 1) * BLOCK]
        acc = jnp.dot(lhs, fine[b, 0], preferred_element_type=F32)
        acc = acc + jnp.dot(lhs, fine[b, 1], preferred_element_type=F32)
        parts.append(fold(acc))
    return vec + jnp.concatenate(parts, axis=1)


def payload_line(base, coarse, dots):
    lane, row = iota((2, 128), 1), iota((2, 128), 0)
    tile = jnp.zeros((2, 128), F32)
    for slot, value in enumerate(coarse):
        tile = jnp.where(lane == row * HALF + base + slot, value, tile)
    for slot, value in enumerate(dots):
        tile = jnp.where(lane == row * HALF + DOTS + slot, value, tile)
    return jnp.sum(tile, axis=0, keepdims=True)


def payload(out, base, coarse, dots):
    out.put(jnp.broadcast_to(payload_line(base, coarse, dots), out.ref.shape))


def restrict(vec, near):
    return [lane_sum(jnp.where(near == float(k), vec, 0.0)) for k in range(NEAR)]


def group_sums(rows_ref, size):
    rows = rows_ref[...]
    return jnp.sum(rows.reshape(rows.shape[0] // size, size, 128), axis=1)


def pick(line, slot):
    lane, row = iota((2, 128), 1), iota((2, 128), 0)
    return lane_sum(jnp.where(lane == row * HALF + DOTS + slot, line, 0.0))


def spread(value):
    return jnp.where(iota((1, 128), 1) < HALF, value[0:1], value[1:2])


def coarse_values(cr_ref, g_ref):
    acc = [jnp.zeros((COLS, 128), F32) for _ in range(4)]
    for g in range(cr_ref.shape[0]):
        acc[g % 4] = acc[g % 4] + g_ref[:, g * 128 : (g + 1) * 128] * cr_ref[g : g + 1, :]
    total = (acc[0] + acc[1]) + (acc[2] + acc[3])
    first = iota((COLS, 128), 1) < HALF
    return lane_sum(jnp.where(first, total, 0.0)), lane_sum(jnp.where(first, 0.0, total))


def prolong(base, aggs, values):
    for k in range(COLS):
        value = jnp.concatenate([v[k : k + 1] for v in values], axis=0)
        base = base + jnp.where(aggs == float(k), value, 0.0)
    return base


def sweep(z_win, tiles, rows_ref, sum_ref):
    src, k_ref, sem = tiles
    rows_ref[...] = stacked(z_win)

    def one(i, carry):
        pltpu.make_async_copy(src.at[i], k_ref.at[i], sem.at[i]).wait()
        at = pl.multiple_of(i * BLOCK, BLOCK)
        lhs = rows_ref[:, pl.ds(at, SPAN * BLOCK)]
        acc = jnp.dot(lhs, k_ref[i], preferred_element_type=F32)
        sum_ref[:, pl.ds(at, BLOCK)] = fold(acc)
        return carry

    lax.fori_loop(0, OWN, one, 0)
    return SHIFT * z_win[:, MID] + KERNEL_SCALE * sum_ref[...]


def start_tiles(tiles):
    src, k_ref, sem = tiles
    for i in range(OWN):
        pltpu.make_async_copy(src.at[i], k_ref.at[i], sem.at[i]).start()


def setup_kernel(subs, me, ins, outs, noise_src, wide, noise, sem):
    arrival = pltpu.make_async_copy(noise_src, noise, sem)
    arrival.start()
    res, agg, coarse, coords = ins
    pay, mine, fine, res_out = outs
    res_out.put(res()[...])
    device = me[0]
    last = pay.ref.shape[1] - 8
    lane_base = 2 * (device % (CORES * subs))
    r = res()[...]
    agg_line = agg()[...].astype(F32)
    near = agg_line - (2 * device - 1).astype(F32)
    line = payload_line(lane_base, restrict(r, near), [])
    rows, centres = coarse.ref.shape
    first_col = device // (CORES * subs) * (2 * CORES * subs) - 4
    first_row = device % subs * rows
    c = coarse()[...]
    sel = (iota((WIDE, centres), 1) == first_col + iota((WIDE, centres), 0)).astype(BF16)
    c_sel = lax.dot_general(sel, c, (((1,), (1,)), ((), ())), preferred_element_type=F32)
    e_sel = (first_row + iota((WIDE, rows), 1) == first_col + iota((WIDE, rows), 0)).astype(F32)
    both = jnp.concatenate([c_sel, e_sel], axis=0).astype(BF16)
    full = jnp.dot(both, c, preferred_element_type=F32)
    full = full[:WIDE] + full[WIDE:]
    extra = c_sel + e_sel
    if wide.shape[1] > centres:
        wide[...] = jnp.zeros_like(wide)
    wide[:, 0:centres] = full
    start = pl.multiple_of(first_row, rows)
    wide[:, pl.ds(start, rows)] = wide[:, pl.ds(start, rows)] + extra
    for slot in range(CORES * subs):
        low = 2 * slot + 1
        for v in range(last // 8):
            piece = wide[low : low + COLS, v * 128 : (v + 1) * 128]
            pay.ref[slot, v * 8 : v * 8 + 8] = piece
        pay.ref[slot, last : last + 8] = jnp.broadcast_to(line, (8, 128))
    arrival.wait()
    for b in range(OWN):
        n = noise[b]
        nt = n.T
        f = jnp.dot(nt, n, precision=HIGHEST, preferred_element_type=F32) + (n + nt)
        fine.ref[b, 0], fine.ref[b, 1] = split2(f)
    mine.ref[0:3] = coords()[...]
    mine.ref[3:4] = agg_line
    mine.ref[4:6] = fine_apply(r, fine.ref)
    mine.ref[6:8] = jnp.zeros((2, POINTS), F32)


def tile_kernel(
    subs, me, pairs, live_count, ins, outs, k_out, k_ref, xyz, tall_xyz, tall, present, k_sem
):
    near_a, near_b, parts, own = ins
    aggs, zb, g_lines = outs
    device = me[0]

    def clear(t, carry):
        present[t] = 0
        return carry

    def mark(s, carry):
        row, col = pairs[0, s], pairs[1, s]
        present[(row - device * OWN) * SPAN + (col - row + REACH)] = 1
        return carry

    lax.fori_loop(0, OWN * SPAN, clear, 0)
    lax.fori_loop(0, live_count[0], mark, 0)
    odd = device % 2 == 1
    a, b = near_a()[...], near_b()[...]
    xyz[:, 0:POINTS] = jnp.where(odd, a, b)
    xyz[:, MID] = own()[...]
    xyz[:, 2 * POINTS : WIN] = jnp.where(odd, b, a)
    aggs.put(xyz[3:4] - (2 * device - 3).astype(F32))
    zb.put(xyz[4:6])

    for j in range(WIN // BLOCK):
        tall_xyz[j * BLOCK : (j + 1) * BLOCK, 0:8] = xyz[:, j * BLOCK : (j + 1) * BLOCK].T

    phase = (iota((STRIP, BLOCK), 0) + iota((STRIP, BLOCK), 1)) % STRIP
    phase = (phase * 7) % STRIP
    dither = 1.0 + (phase.astype(F32) - (STRIP - 1) / 2) * (2.0**-7 / STRIP)
    five, four = 5.0 * dither, 4.0 * dither

    def one(t, carry):
        i = t // SPAN
        o = t - i * SPAN
        live = present[t]
        spot = pl.ds(pl.multiple_of(o * BLOCK, BLOCK), BLOCK)

        @pl.when(live > 0)
        def _():
            row = xyz[0:3, pl.ds(pl.multiple_of((i + REACH) * BLOCK, BLOCK), BLOCK)]
            rows = [jnp.broadcast_to(row[c : c + 1], (STRIP, BLOCK)) for c in range(3)]

            def strip(s, carry):
                at = pl.multiple_of((i + o) * BLOCK + s * STRIP, STRIP)
                col = tall_xyz[pl.ds(at, STRIP), 0:8]
                d2 = (col[:, 0:1] - rows[0]) ** 2
                d2 = d2 + (col[:, 1:2] - rows[1]) ** 2
                d2 = d2 + (col[:, 2:3] - rows[2]) ** 2
                dist = d2 * lax.rsqrt(jnp.maximum(d2, 1e-30))
                fall = jnp.maximum(1.0 - dist, 0.0)
                square = fall * fall
                value = (square * square) * (five - four * fall)
                to = pl.ds(pl.multiple_of(o * BLOCK + s * STRIP, STRIP), STRIP)
                k_ref[i, to] = value.astype(BF16)
                return carry

            lax.fori_loop(0, BLOCK // STRIP, strip, 0, unroll=True)

        @pl.when(live == 0)
        def _():
            zero = jnp.zeros((BLOCK, BLOCK), BF16)
            k_ref[i, spot] = zero

        @pl.when(o == SPAN - 1)
        def _():
            pltpu.make_async_copy(k_ref.at[i], k_out.at[i], k_sem.at[i]).start()

        return carry

    lax.fori_loop(0, OWN * SPAN, one, 0)
    zero = jnp.zeros((COLS, 128), F32)
    span = tall.shape[1] - 256
    tall[:, 0:128] = zero
    for v in range(span // 128):
        total = parts.ref[0, v * 8 : v * 8 + 8]
        for s in range(1, subs):
            total = total + parts.ref[s, v * 8 : v * 8 + 8]
        tall[:, 128 + v * 128 : 256 + v * 128] = total * (AGG ** (-0.5))
    tall[:, 128 + span :] = zero
    lane = iota((COLS, 128), 1)
    step = 2 * CORES * subs
    count = step + 2
    for g in range(g_lines.ref.shape[1] // 128):
        at = 128 + step * g - 1
        lo, off = at // 128 * 128, at % 128
        line = tall[:, lo : lo + 128]
        if off:
            line = pltpu.roll(line, 128 - off, 1)
        if off + count > 128:
            after = pltpu.roll(tall[:, lo + 128 : lo + 256], 128 - off, 1)
            line = jnp.where(lane < 128 - off, line, after)
        line = jnp.where(lane < count, line, 0.0)
        g_lines.ref[:, g * 128 : (g + 1) * 128] = line + pltpu.roll(line, HALF, 1)
    for i in range(OWN):
        pltpu.make_async_copy(k_ref.at[i], k_out.at[i], k_sem.at[i]).wait()


def first_kernel(subs, me, ins, outs, k_src, k_ref, rows_ref, sum_ref, k_sem):
    gath, g_lines, zb, aggs, res, fine = ins
    z_out, w_out, pay, mw_out, cr_out = outs
    tiles = (k_src, k_ref, k_sem)
    start_tiles(tiles)
    device = me[0]
    cr_out.put(gath()[...])
    g_lines()
    z_win = prolong(zb()[...], aggs()[...], coarse_values(gath.ref, g_lines.ref))
    z = z_win[:, MID]
    z_out.put(z)
    w = sweep(z_win, tiles, rows_ref, sum_ref)
    w_out.put(w)
    mw_out.put(fine_apply(w, fine()))
    near = aggs.ref[:, MID] - 2.0
    dots = [lane_sum(res()[...] * z), lane_sum(z * w)]
    payload(pay, 2 * (device % (CORES * subs)), restrict(w, near), dots)


def step_kernel(subs, first, last, extra, me, ins, outs, *raw):
    ins, outs = list(ins), list(outs)
    device = me[0]
    take = lambda k: [ins.pop(0) for _ in range(k)]
    give = lambda k: [outs.pop(0) for _ in range(k)]
    (gath,) = take(1)
    near_mw = [] if last else take(2)
    z, w, x, r, cr, mw_o, zb, aggs, g_lines = take(9)
    d_old = q_old = crq_old = mq_old = rz_old = curve_old = None
    if not first:
        rz_old, curve_old, d_old, q_old, crq_old, mq_old = take(6)
    if last:
        (coarse,) = take(1)
        (vec_ref,) = raw
        x_out, r_out, d_out, z_out, rz_out, fine_out, cr_out, pay = give(8)
    else:
        x_out, r_out, d_out, q_out, rz_out, curve_out, crq_out, mq_out = give(8)
        cr_out, zb_out, z_out, w_out, mw_out, pay = give(6)
        (fine,) = take(1)
        k_src, k_ref, rows_ref, sum_ref, k_sem = raw
        tiles = (k_src, k_ref, k_sem)
        start_tiles(tiles)

    got = group_sums(gath.ref, CORES * subs)
    total = jnp.sum(got, axis=0, keepdims=True)
    rz, zw = pick(total, 0), pick(total, 1)
    mw = mw_o()[...]
    if not last:
        odd = device % 2 == 1
        a, b = [item()[...] for item in near_mw]
        mw = jnp.concatenate([jnp.where(odd, a, b), mw, jnp.where(odd, b, a)], axis=1)
    if first:
        curve = zw
        d, q, crq, mq = z()[...], w()[...], got, mw
    else:
        beta = rz / rz_old()[:, 0:1]
        curve = zw + beta * (2.0 * pick(total, 2) + beta * curve_old()[:, 0:1])
        d = z()[...] + beta * d_old()[...]
        q = w()[...] + beta * q_old()[...]
        crq = got + spread(beta) * crq_old()[...]
        mq = mw + beta * (mq_old()[:, MID] if last else mq_old()[...])
    alpha = rz / curve
    r_new = r()[...] - alpha * q
    x_out.put(alpha * d if first else x()[...] + alpha * d)
    r_out.put(r_new)
    d_out.put(d)
    rz_out.put(jnp.broadcast_to(rz, rz_out.ref.shape))
    cr_new = cr()[...] - spread(alpha) * crq
    zb_new = (zb()[:, MID] if last else zb()[...]) - alpha * mq
    cr_out.put(cr_new)
    values = coarse_values(cr_out.ref, g_lines())
    if last:
        z_new = prolong(zb_new, aggs()[:, MID], values)
        z_out.put(z_new)
        e = [pick(total, 3 + i) for i in range(6)]
        linear = e[1] + beta * e[2]
        square = e[3] + beta * (2.0 * e[4] + beta * e[5])
        fine = e[0] + alpha * (alpha * square - 2.0 * linear)
        fine_out.put(jnp.broadcast_to(fine, fine_out.ref.shape))
        lay_out(cr_out.ref, vec_ref, 2 * CORES * subs)
        rows, centres = coarse.ref.shape
        lhs = stacked(vec_ref[:, 128 : 128 + centres])
        y = fold(
            lax.dot_general(
                lhs, coarse()[...], (((1,), (1,)), ((), ())), preferred_element_type=F32
            )
        )
        start = pl.multiple_of(device % subs * rows, rows)
        y = y + vec_ref[:, pl.ds(128 + start, rows)]
        payload(pay, 0, [], [lane_sum(y * y) * (AGG ** (-0.5))])
        return
    zb_out.put(zb_new)
    q_out.put(q)
    crq_out.put(crq)
    mq_out.put(mq)
    curve_out.put(jnp.broadcast_to(curve, curve_out.ref.shape))
    z_win = prolong(zb_new, aggs()[...], values)
    z_new = z_win[:, MID]
    z_out.put(z_new)
    w_new = sweep(z_win, tiles, rows_ref, sum_ref)
    w_out.put(w_new)
    mw_out.put(fine_apply(w_new, fine()))
    dots = [lane_sum(r_new * z_new), lane_sum(z_new * w_new), lane_sum(z_new * q)]
    if extra:
        zb_mid, mw_new, mq_mid = zb_new[:, MID], mw_out.ref[...], mq[:, MID]
        pairs = [(r_new, zb_mid), (w_new, zb_mid), (q, zb_mid)]
        pairs = pairs + [(w_new, mw_new), (w_new, mq_mid), (q, mq_mid)]
        dots = dots + [lane_sum(a * b) for a, b in pairs]
    near = aggs.ref[:, MID] - 2.0
    payload(pay, 2 * (device % (CORES * subs)), restrict(w_new, near), dots)


def lay_out(cr_ref, vec_ref, step):
    lane = iota((1, 128), 1)
    zero = jnp.zeros((1, 128), F32)
    sums = [[zero] * (vec_ref.shape[1] // 128) for _ in range(2)]
    for g in range(cr_ref.shape[0]):
        at = 128 + step * g - 1
        v, off = at // 128, at % 128
        line = cr_ref[g : g + 1, :]
        end = off + step + 2
        for f in range(2):
            moved = pltpu.roll(line, (off + f * HALF) % 128, 1)
            here = (lane >= off) & (lane < end)
            sums[f][v] = sums[f][v] + jnp.where(here, moved, 0.0)
            if end > 128:
                sums[f][v + 1] = sums[f][v + 1] + jnp.where(lane < end - 128, moved, 0.0)
    for v in range(len(sums[0])):
        both = jnp.concatenate([sums[0][v], sums[1][v]], axis=0)
        vec_ref[:, v * 128 : (v + 1) * 128] = both


def last_kernel(ins, outs):
    coarse, z, d_old, rz_old, fine = ins
    (d_out,) = outs
    total = jnp.sum(coarse()[...], axis=0, keepdims=True)
    beta = (pick(total, 0) + fine()[:, 0:1]) / rz_old()[:, 0:1]
    d_out.put(z()[...] + beta * d_old()[...])


def neighbours(block):
    count = lax.axis_size(AXES)
    inner = [(i, i ^ 1) for i in range(count)]
    outer = [(i, i + 1) for i in range(1, count - 1, 2)]
    outer = outer + [(i + 1, i) for i in range(1, count - 1, 2)]
    return lax.ppermute(block, AXES, inner), lax.ppermute(block, AXES, outer)


def first_stage(rows):
    return lax.all_to_all(rows, ("core", "sub"), 0, 0, tiled=True)


def second_stage(near):
    groups = lax.axis_size("grp")
    total = jnp.broadcast_to(jnp.sum(near, axis=0, keepdims=True), (groups, 128))
    return lax.all_to_all(total, "grp", 0, 0, tiled=True)


def per_device(coords, right_side, tile_pairs, tile_count, fine_noise, coarse_noise, aggregate):
    fields = right_side.shape[0]
    subs, groups = lax.axis_size("sub"), lax.axis_size("grp")
    centres = coarse_noise.shape[1]
    device = (lax.axis_index("grp") * CORES + lax.axis_index("core")) * subs
    me = jnp.full((1,), device + lax.axis_index("sub"), jnp.int32)
    vec, win = ((fields, POINTS), F32), ((fields, WIN), F32)
    line, small = ((groups, 128), F32), ((fields, 128), F32)
    row = ((CORES * subs * groups, 128), F32)
    tiles = ((OWN, SPAN * BLOCK, BLOCK), BF16)
    fines = ((OWN, 2, BLOCK, BLOCK), BF16)
    lines = ((COLS, groups * 128), F32)
    sweeping = [
        pltpu.VMEM(*tiles),
        pltpu.VMEM((3 * fields, WIN), BF16),
        pltpu.VMEM(*vec),
        pltpu.SemaphoreType.DMA((OWN,)),
    ]

    span = max(centres, 128)
    pay, mine, fine, res = call(
        functools.partial(setup_kernel, subs),
        [((CORES * subs, span // 16 + 8, 128), F32), ((8, POINTS), F32), fines, vec],
        raw=[fine_noise],
        scratch=[
            pltpu.VMEM((WIDE, span), F32),
            pltpu.VMEM(fine_noise.shape, F32),
            pltpu.SemaphoreType.DMA,
        ],
        smem=1,
        limit=SETUP_LIMIT,
    )(me, right_side, aggregate[None], coarse_noise, coords)
    near_a, near_b = neighbours(mine)
    parts = first_stage(pay)
    got = second_stage(parts[:, span // 16])
    aggs, zb, g_lines, kernel_tiles = call(
        functools.partial(tile_kernel, subs),
        [((1, WIN), F32), win, lines],
        raw_outs=[tiles],
        scratch=[
            pltpu.VMEM(*tiles),
            pltpu.VMEM((8, WIN), F32),
            pltpu.VMEM((WIN, 8), F32),
            pltpu.VMEM((COLS, span + 256), F32),
            pltpu.SMEM((OWN * SPAN,), jnp.int32),
            pltpu.SemaphoreType.DMA((OWN,)),
        ],
        smem=3,
    )(me, tile_pairs, tile_count, near_a, near_b, parts, mine)

    z, w, pay, mw, cr = call(
        functools.partial(first_kernel, subs),
        [vec, vec, row, vec, line],
        raw=[kernel_tiles],
        scratch=sweeping,
        smem=1,
    )(me, got, g_lines, zb, aggs, res, fine)
    x, r = res, res
    old = ()
    for iteration in range(ITERS):
        first, last = iteration == 0, iteration == ITERS - 1
        got = lax.all_to_all(pay, AXES, 0, 0, tiled=True)
        state = (z, w, x, r, cr, mw, zb, aggs, g_lines)
        body = functools.partial(step_kernel, subs, first, last, iteration == ITERS - 2)
        if last:
            outs = [vec, vec, vec, vec, small, small, line, ((subs, 128), F32)]
            room = [pltpu.VMEM((fields, span + 256), F32)]
            run = call(body, outs, scratch=room, smem=1)
            x, r, d, z, rz, fine_rz, _, pay = run(me, got, *state, *old, coarse_noise)
        else:
            outs = [vec] * 4 + [small, small, line, win, line, win, vec, vec, vec, row]
            run = call(body, outs, raw=[kernel_tiles], scratch=sweeping, smem=1)
            x, r, d, q, rz, curve, crq, mq, cr, zb, z, w, mw, pay = run(
                me, got, *neighbours(mw), *state, *old, fine
            )
            old = (rz, curve, d, q, crq, mq)
    coarse_rz = lax.all_to_all(pay, "sub", 0, 0, tiled=True)
    (d,) = call(last_kernel, [vec])(coarse_rz, z, d, rz, fine_rz)
    return (x, r, d)


def solution(mesh):
    devices = mesh.devices
    blk, subs = devices.shape
    fine_mesh = Mesh(devices.reshape(blk // CORES, CORES, subs), AXES)
    points = P(None, AXES)
    in_specs = (
        points,
        points,
        points,
        P(AXES),
        P(AXES, None, None),
        P("sub", None),
        P(AXES),
    )
    return jax.shard_map(
        per_device, mesh=fine_mesh, in_specs=in_specs, out_specs=(points,) * 3, check_vma=False
    )
```

```python
import functools

import jax
import jax.numpy as jnp
from jax import lax
from jax.experimental import pallas as pl
from jax.experimental.pallas import tpu as pltpu
from jax.sharding import Mesh
from jax.sharding import PartitionSpec as P

BLOCK = 256
REACH = 4
AGG = 512
ITERS = 4
SHIFT = 1.5
KERNEL_SCALE = 1.0 / (BLOCK * (2 * REACH + 1))
OWN = 4
POINTS = OWN * BLOCK
WIN = 3 * POINTS
MID = slice(POINTS, 2 * POINTS)
SPAN = 2 * REACH + 1
HALF = 64
DOTS = 32
NEAR = 4
COLS = 8
WIDE = 32
CORES = 2
STRIP = 16
AXES = ("grp", "core", "sub")
VMEM_LIMIT = 50 * 1024 * 1024
SETUP_LIMIT = 52 * 1024 * 1024
F32 = jnp.float32
BF16 = jnp.bfloat16
HIGHEST = lax.Precision.HIGHEST


class Operand:
    def __init__(self, ref):
        self.ref = ref

    def __call__(self):
        return self.ref

    def put(self, value):
        self.ref[...] = value


def call(body, outs, raw=(), raw_outs=(), scratch=(), smem=0, limit=None):
    def run(*args):
        n, m = len(args) - smem, len(outs)
        p, q = len(raw), len(raw_outs)

        def kernel(*refs):
            refs = list(refs)
            take = lambda k: [refs.pop(0) for _ in range(k)]
            scalars, ins, raw_in = take(smem), take(n), take(p)
            results, raw_out = take(m), take(q)
            body(
                *scalars,
                [Operand(ref) for ref in ins],
                [Operand(ref) for ref in results],
                *raw_in,
                *raw_out,
                *refs,
            )

        smem_spec = pl.BlockSpec(memory_space=pltpu.SMEM)
        vmem_spec = pl.BlockSpec(memory_space=pltpu.VMEM)
        hbm_spec = pl.BlockSpec(memory_space=pltpu.HBM)
        return pl.pallas_call(
            kernel,
            out_shape=[jax.ShapeDtypeStruct(s, d) for s, d in list(outs) + list(raw_outs)],
            in_specs=[smem_spec] * smem + [vmem_spec] * n + [hbm_spec] * p,
            out_specs=[vmem_spec] * m + [hbm_spec] * q,
            scratch_shapes=list(scratch),
            compiler_params=pltpu.CompilerParams(vmem_limit_bytes=limit or VMEM_LIMIT),
        )(*args, *raw)

    return run


def iota(shape, dim):
    return lax.broadcasted_iota(jnp.int32, shape, dim)


def split2(x):
    hi = x.astype(BF16)
    return hi, (x - hi.astype(F32)).astype(BF16)


def stacked(x):
    hi = x.astype(BF16).astype(F32)
    rest = x - hi
    mid = rest.astype(BF16).astype(F32)
    return jnp.concatenate([hi, mid, rest - mid], axis=0).astype(BF16)


def fold(acc):
    return acc[0:2] + acc[2:4] + acc[4:6]


def lane_sum(x):
    return jnp.sum(x, axis=1, keepdims=True)


def fine_apply(vec, fine):
    rows = stacked(vec)
    parts = []
    for b in range(OWN):
        lhs = rows[:, b * BLOCK : (b + 1) * BLOCK]
        acc = jnp.dot(lhs, fine[b, 0], preferred_element_type=F32)
        acc = acc + jnp.dot(lhs, fine[b, 1], preferred_element_type=F32)
        parts.append(fold(acc))
    return vec + jnp.concatenate(parts, axis=1)


def payload_line(base, coarse, dots):
    lane, row = iota((2, 128), 1), iota((2, 128), 0)
    tile = jnp.zeros((2, 128), F32)
    for slot, value in enumerate(coarse):
        tile = jnp.where(lane == row * HALF + base + slot, value, tile)
    for slot, value in enumerate(dots):
        tile = jnp.where(lane == row * HALF + DOTS + slot, value, tile)
    return jnp.sum(tile, axis=0, keepdims=True)


def payload(out, base, coarse, dots):
    out.put(jnp.broadcast_to(payload_line(base, coarse, dots), out.ref.shape))


def restrict(vec, near):
    return [lane_sum(jnp.where(near == float(k), vec, 0.0)) for k in range(NEAR)]


def group_sums(rows_ref, size):
    rows = rows_ref[...]
    return jnp.sum(rows.reshape(rows.shape[0] // size, size, 128), axis=1)


def pick(line, slot):
    lane, row = iota((2, 128), 1), iota((2, 128), 0)
    return lane_sum(jnp.where(lane == row * HALF + DOTS + slot, line, 0.0))


def spread(value):
    return jnp.where(iota((1, 128), 1) < HALF, value[0:1], value[1:2])


def coarse_values(cr_ref, g_ref):
    acc = [jnp.zeros((COLS, 128), F32) for _ in range(4)]
    for g in range(cr_ref.shape[0]):
        acc[g % 4] = acc[g % 4] + g_ref[:, g * 128 : (g + 1) * 128] * cr_ref[g : g + 1, :]
    total = (acc[0] + acc[1]) + (acc[2] + acc[3])
    first = iota((COLS, 128), 1) < HALF
    return lane_sum(jnp.where(first, total, 0.0)), lane_sum(jnp.where(first, 0.0, total))


def prolong(base, aggs, values):
    for k in range(COLS):
        value = jnp.concatenate([v[k : k + 1] for v in values], axis=0)
        base = base + jnp.where(aggs == float(k), value, 0.0)
    return base


def sweep(z_win, tiles, rows_ref, sum_ref):
    src, k_ref, sem = tiles
    rows_ref[...] = stacked(z_win)

    def one(i, carry):
        pltpu.make_async_copy(src.at[i], k_ref.at[i], sem.at[i]).wait()
        at = pl.multiple_of(i * BLOCK, BLOCK)
        lhs = rows_ref[:, pl.ds(at, SPAN * BLOCK)]
        acc = jnp.dot(lhs, k_ref[i], preferred_element_type=F32)
        sum_ref[:, pl.ds(at, BLOCK)] = fold(acc)
        return carry

    lax.fori_loop(0, OWN, one, 0)
    return SHIFT * z_win[:, MID] + KERNEL_SCALE * sum_ref[...]


def start_tiles(tiles):
    src, k_ref, sem = tiles
    for i in range(OWN):
        pltpu.make_async_copy(src.at[i], k_ref.at[i], sem.at[i]).start()


def setup_kernel(subs, me, ins, outs, noise_src, wide, noise, sem):
    arrival = pltpu.make_async_copy(noise_src, noise, sem)
    arrival.start()
    res, agg, coarse, coords = ins
    pay, mine, fine, res_out = outs
    res_out.put(res()[...])
    device = me[0]
    last = pay.ref.shape[1] - 8
    lane_base = 2 * (device % (CORES * subs))
    r = res()[...]
    agg_line = agg()[...].astype(F32)
    near = agg_line - (2 * device - 1).astype(F32)
    line = payload_line(lane_base, restrict(r, near), [])
    rows, centres = coarse.ref.shape
    first_col = device // (CORES * subs) * (2 * CORES * subs) - 4
    first_row = device % subs * rows
    c = coarse()[...]
    sel = (iota((WIDE, centres), 1) == first_col + iota((WIDE, centres), 0)).astype(BF16)
    c_sel = lax.dot_general(sel, c, (((1,), (1,)), ((), ())), preferred_element_type=F32)
    e_sel = (first_row + iota((WIDE, rows), 1) == first_col + iota((WIDE, rows), 0)).astype(F32)
    both = jnp.concatenate([c_sel, e_sel], axis=0).astype(BF16)
    full = jnp.dot(both, c, preferred_element_type=F32)
    full = full[:WIDE] + full[WIDE:]
    extra = c_sel + e_sel
    if wide.shape[1] > centres:
        wide[...] = jnp.zeros_like(wide)
    wide[:, 0:centres] = full
    start = pl.multiple_of(first_row, rows)
    wide[:, pl.ds(start, rows)] = wide[:, pl.ds(start, rows)] + extra
    for slot in range(CORES * subs):
        low = 2 * slot + 1
        for v in range(last // 8):
            piece = wide[low : low + COLS, v * 128 : (v + 1) * 128]
            pay.ref[slot, v * 8 : v * 8 + 8] = piece
        pay.ref[slot, last : last + 8] = jnp.broadcast_to(line, (8, 128))
    arrival.wait()
    for b in range(OWN):
        n = noise[b]
        nt = n.T
        f = jnp.dot(nt, n, precision=HIGHEST, preferred_element_type=F32) + (n + nt)
        fine.ref[b, 0], fine.ref[b, 1] = split2(f)
    mine.ref[0:3] = coords()[...]
    mine.ref[3:4] = agg_line
    mine.ref[4:6] = fine_apply(r, fine.ref)
    mine.ref[6:8] = jnp.zeros((2, POINTS), F32)


def tile_kernel(
    subs, me, pairs, live_count, ins, outs, k_out, k_ref, xyz, tall_xyz, tall, present, k_sem
):
    near_a, near_b, parts, own = ins
    aggs, zb, g_lines = outs
    device = me[0]

    def clear(t, carry):
        present[t] = 0
        return carry

    def mark(s, carry):
        row, col = pairs[0, s], pairs[1, s]
        present[(row - device * OWN) * SPAN + (col - row + REACH)] = 1
        return carry

    lax.fori_loop(0, OWN * SPAN, clear, 0)
    lax.fori_loop(0, live_count[0], mark, 0)
    odd = device % 2 == 1
    a, b = near_a()[...], near_b()[...]
    xyz[:, 0:POINTS] = jnp.where(odd, a, b)
    xyz[:, MID] = own()[...]
    xyz[:, 2 * POINTS : WIN] = jnp.where(odd, b, a)
    aggs.put(xyz[3:4] - (2 * device - 3).astype(F32))
    zb.put(xyz[4:6])

    for j in range(WIN // BLOCK):
        at = slice(j * BLOCK, (j + 1) * BLOCK)
        tall_xyz[0, at, :] = xyz[:, at].T
        for c in range(1, 3):
            tall_xyz[c, at, :] = jnp.concatenate([xyz[c:8, at], xyz[0:c, at]], axis=0).T

    phase = (iota((STRIP, BLOCK), 0) + iota((STRIP, BLOCK), 1)) % STRIP
    phase = (phase * 7) % STRIP
    dither = 1.0 + (phase.astype(F32) - (STRIP - 1) / 2) * (2.0**-7 / STRIP)
    five, four = 5.0 * dither, 4.0 * dither

    def one(t, carry):
        i = t // SPAN
        o = t - i * SPAN
        live = present[t]
        spot = pl.ds(pl.multiple_of(o * BLOCK, BLOCK), BLOCK)

        @pl.when(live > 0)
        def _():
            row = xyz[0:3, pl.ds(pl.multiple_of((i + REACH) * BLOCK, BLOCK), BLOCK)]
            rows = [jnp.broadcast_to(row[c : c + 1], (STRIP, BLOCK)) for c in range(3)]

            def strip(s, carry):
                at = pl.multiple_of((i + o) * BLOCK + s * STRIP, STRIP)
                cols = [tall_xyz[c, pl.ds(at, STRIP), 0:1] for c in range(3)]
                d2 = (cols[0] - rows[0]) ** 2
                d2 = d2 + (cols[1] - rows[1]) ** 2
                d2 = d2 + (cols[2] - rows[2]) ** 2
                dist = d2 * lax.rsqrt(jnp.maximum(d2, 1e-30))
                fall = jnp.maximum(1.0 - dist, 0.0)
                square = fall * fall
                value = (square * square) * (five - four * fall)
                to = pl.ds(pl.multiple_of(o * BLOCK + s * STRIP, STRIP), STRIP)
                k_ref[i, to] = value.astype(BF16)
                return carry

            lax.fori_loop(0, BLOCK // STRIP, strip, 0, unroll=True)

        @pl.when(live == 0)
        def _():
            zero = jnp.zeros((BLOCK, BLOCK), BF16)
            k_ref[i, spot] = zero

        @pl.when(o == SPAN - 1)
        def _():
            pltpu.make_async_copy(k_ref.at[i], k_out.at[i], k_sem.at[i]).start()

        return carry

    lax.fori_loop(0, OWN * SPAN, one, 0)
    zero = jnp.zeros((COLS, 128), F32)
    span = tall.shape[1] - 256
    tall[:, 0:128] = zero
    for v in range(span // 128):
        total = parts.ref[0, v * 8 : v * 8 + 8]
        for s in range(1, subs):
            total = total + parts.ref[s, v * 8 : v * 8 + 8]
        tall[:, 128 + v * 128 : 256 + v * 128] = total * (AGG ** (-0.5))
    tall[:, 128 + span :] = zero
    lane = iota((COLS, 128), 1)
    step = 2 * CORES * subs
    count = step + 2
    for g in range(g_lines.ref.shape[1] // 128):
        at = 128 + step * g - 1
        lo, off = at // 128 * 128, at % 128
        line = tall[:, lo : lo + 128]
        if off:
            line = pltpu.roll(line, 128 - off, 1)
        if off + count > 128:
            after = pltpu.roll(tall[:, lo + 128 : lo + 256], 128 - off, 1)
            line = jnp.where(lane < 128 - off, line, after)
        line = jnp.where(lane < count, line, 0.0)
        g_lines.ref[:, g * 128 : (g + 1) * 128] = line + pltpu.roll(line, HALF, 1)
    for i in range(OWN):
        pltpu.make_async_copy(k_ref.at[i], k_out.at[i], k_sem.at[i]).wait()


def first_kernel(subs, me, ins, outs, k_src, k_ref, rows_ref, sum_ref, k_sem):
    gath, g_lines, zb, aggs, res, fine = ins
    z_out, w_out, pay, mw_out, cr_out = outs
    tiles = (k_src, k_ref, k_sem)
    start_tiles(tiles)
    device = me[0]
    cr_out.put(gath()[...])
    g_lines()
    z_win = prolong(zb()[...], aggs()[...], coarse_values(gath.ref, g_lines.ref))
    z = z_win[:, MID]
    z_out.put(z)
    w = sweep(z_win, tiles, rows_ref, sum_ref)
    w_out.put(w)
    mw_out.put(fine_apply(w, fine()))
    near = aggs.ref[:, MID] - 2.0
    dots = [lane_sum(res()[...] * z), lane_sum(z * w)]
    payload(pay, 2 * (device % (CORES * subs)), restrict(w, near), dots)


def step_kernel(subs, first, last, extra, me, ins, outs, *raw):
    ins, outs = list(ins), list(outs)
    device = me[0]
    take = lambda k: [ins.pop(0) for _ in range(k)]
    give = lambda k: [outs.pop(0) for _ in range(k)]
    (gath,) = take(1)
    near_mw = [] if last else take(2)
    z, w, x, r, cr, mw_o, zb, aggs, g_lines = take(9)
    d_old = q_old = crq_old = mq_old = rz_old = curve_old = None
    if not first:
        rz_old, curve_old, d_old, q_old, crq_old, mq_old = take(6)
    if last:
        (coarse,) = take(1)
        (vec_ref,) = raw
        x_out, r_out, d_out, z_out, rz_out, fine_out, cr_out, pay = give(8)
    else:
        x_out, r_out, d_out, q_out, rz_out, curve_out, crq_out, mq_out = give(8)
        cr_out, zb_out, z_out, w_out, mw_out, pay = give(6)
        (fine,) = take(1)
        k_src, k_ref, rows_ref, sum_ref, k_sem = raw
        tiles = (k_src, k_ref, k_sem)
        start_tiles(tiles)

    got = group_sums(gath.ref, CORES * subs)
    total = jnp.sum(got, axis=0, keepdims=True)
    rz, zw = pick(total, 0), pick(total, 1)
    mw = mw_o()[...]
    if not last:
        odd = device % 2 == 1
        a, b = [item()[...] for item in near_mw]
        mw = jnp.concatenate([jnp.where(odd, a, b), mw, jnp.where(odd, b, a)], axis=1)
    if first:
        curve = zw
        d, q, crq, mq = z()[...], w()[...], got, mw
    else:
        beta = rz / rz_old()[:, 0:1]
        curve = zw + beta * (2.0 * pick(total, 2) + beta * curve_old()[:, 0:1])
        d = z()[...] + beta * d_old()[...]
        q = w()[...] + beta * q_old()[...]
        crq = got + spread(beta) * crq_old()[...]
        mq = mw + beta * (mq_old()[:, MID] if last else mq_old()[...])
    alpha = rz / curve
    r_new = r()[...] - alpha * q
    x_out.put(alpha * d if first else x()[...] + alpha * d)
    r_out.put(r_new)
    d_out.put(d)
    rz_out.put(jnp.broadcast_to(rz, rz_out.ref.shape))
    cr_new = cr()[...] - spread(alpha) * crq
    zb_new = (zb()[:, MID] if last else zb()[...]) - alpha * mq
    cr_out.put(cr_new)
    values = coarse_values(cr_out.ref, g_lines())
    if last:
        z_new = prolong(zb_new, aggs()[:, MID], values)
        z_out.put(z_new)
        e = [pick(total, 3 + i) for i in range(6)]
        linear = e[1] + beta * e[2]
        square = e[3] + beta * (2.0 * e[4] + beta * e[5])
        fine = e[0] + alpha * (alpha * square - 2.0 * linear)
        fine_out.put(jnp.broadcast_to(fine, fine_out.ref.shape))
        lay_out(cr_out.ref, vec_ref, 2 * CORES * subs)
        rows, centres = coarse.ref.shape
        lhs = stacked(vec_ref[:, 128 : 128 + centres])
        y = fold(
            lax.dot_general(
                lhs, coarse()[...], (((1,), (1,)), ((), ())), preferred_element_type=F32
            )
        )
        start = pl.multiple_of(device % subs * rows, rows)
        y = y + vec_ref[:, pl.ds(128 + start, rows)]
        payload(pay, 0, [], [lane_sum(y * y) * (AGG ** (-0.5))])
        return
    zb_out.put(zb_new)
    q_out.put(q)
    crq_out.put(crq)
    mq_out.put(mq)
    curve_out.put(jnp.broadcast_to(curve, curve_out.ref.shape))
    z_win = prolong(zb_new, aggs()[...], values)
    z_new = z_win[:, MID]
    z_out.put(z_new)
    w_new = sweep(z_win, tiles, rows_ref, sum_ref)
    w_out.put(w_new)
    mw_out.put(fine_apply(w_new, fine()))
    dots = [lane_sum(r_new * z_new), lane_sum(z_new * w_new), lane_sum(z_new * q)]
    if extra:
        zb_mid, mw_new, mq_mid = zb_new[:, MID], mw_out.ref[...], mq[:, MID]
        pairs = [(r_new, zb_mid), (w_new, zb_mid), (q, zb_mid)]
        pairs = pairs + [(w_new, mw_new), (w_new, mq_mid), (q, mq_mid)]
        dots = dots + [lane_sum(a * b) for a, b in pairs]
    near = aggs.ref[:, MID] - 2.0
    payload(pay, 2 * (device % (CORES * subs)), restrict(w_new, near), dots)


def lay_out(cr_ref, vec_ref, step):
    lane = iota((1, 128), 1)
    zero = jnp.zeros((1, 128), F32)
    sums = [[zero] * (vec_ref.shape[1] // 128) for _ in range(2)]
    for g in range(cr_ref.shape[0]):
        at = 128 + step * g - 1
        v, off = at // 128, at % 128
        line = cr_ref[g : g + 1, :]
        end = off + step + 2
        for f in range(2):
            moved = pltpu.roll(line, (off + f * HALF) % 128, 1)
            here = (lane >= off) & (lane < end)
            sums[f][v] = sums[f][v] + jnp.where(here, moved, 0.0)
            if end > 128:
                sums[f][v + 1] = sums[f][v + 1] + jnp.where(lane < end - 128, moved, 0.0)
    for v in range(len(sums[0])):
        both = jnp.concatenate([sums[0][v], sums[1][v]], axis=0)
        vec_ref[:, v * 128 : (v + 1) * 128] = both


def last_kernel(ins, outs):
    coarse, z, d_old, rz_old, fine = ins
    (d_out,) = outs
    total = jnp.sum(coarse()[...], axis=0, keepdims=True)
    beta = (pick(total, 0) + fine()[:, 0:1]) / rz_old()[:, 0:1]
    d_out.put(z()[...] + beta * d_old()[...])


def neighbours(block):
    count = lax.axis_size(AXES)
    inner = [(i, i ^ 1) for i in range(count)]
    outer = [(i, i + 1) for i in range(1, count - 1, 2)]
    outer = outer + [(i + 1, i) for i in range(1, count - 1, 2)]
    return lax.ppermute(block, AXES, inner), lax.ppermute(block, AXES, outer)


def first_stage(rows):
    return lax.all_to_all(rows, ("core", "sub"), 0, 0, tiled=True)


def second_stage(near):
    groups = lax.axis_size("grp")
    total = jnp.broadcast_to(jnp.sum(near, axis=0, keepdims=True), (groups, 128))
    return lax.all_to_all(total, "grp", 0, 0, tiled=True)


def per_device(coords, right_side, tile_pairs, tile_count, fine_noise, coarse_noise, aggregate):
    fields = right_side.shape[0]
    subs, groups = lax.axis_size("sub"), lax.axis_size("grp")
    centres = coarse_noise.shape[1]
    device = (lax.axis_index("grp") * CORES + lax.axis_index("core")) * subs
    me = jnp.full((1,), device + lax.axis_index("sub"), jnp.int32)
    vec, win = ((fields, POINTS), F32), ((fields, WIN), F32)
    line, small = ((groups, 128), F32), ((fields, 128), F32)
    row = ((CORES * subs * groups, 128), F32)
    tiles = ((OWN, SPAN * BLOCK, BLOCK), BF16)
    fines = ((OWN, 2, BLOCK, BLOCK), BF16)
    lines = ((COLS, groups * 128), F32)
    sweeping = [
        pltpu.VMEM(*tiles),
        pltpu.VMEM((3 * fields, WIN), BF16),
        pltpu.VMEM(*vec),
        pltpu.SemaphoreType.DMA((OWN,)),
    ]

    span = max(centres, 128)
    pay, mine, fine, res = call(
        functools.partial(setup_kernel, subs),
        [((CORES * subs, span // 16 + 8, 128), F32), ((8, POINTS), F32), fines, vec],
        raw=[fine_noise],
        scratch=[
            pltpu.VMEM((WIDE, span), F32),
            pltpu.VMEM(fine_noise.shape, F32),
            pltpu.SemaphoreType.DMA,
        ],
        smem=1,
        limit=SETUP_LIMIT,
    )(me, right_side, aggregate[None], coarse_noise, coords)
    near_a, near_b = neighbours(mine)
    parts = first_stage(pay)
    got = second_stage(parts[:, span // 16])
    aggs, zb, g_lines, kernel_tiles = call(
        functools.partial(tile_kernel, subs),
        [((1, WIN), F32), win, lines],
        raw_outs=[tiles],
        scratch=[
            pltpu.VMEM(*tiles),
            pltpu.VMEM((8, WIN), F32),
            pltpu.VMEM((3, WIN, 8), F32),
            pltpu.VMEM((COLS, span + 256), F32),
            pltpu.SMEM((OWN * SPAN,), jnp.int32),
            pltpu.SemaphoreType.DMA((OWN,)),
        ],
        smem=3,
    )(me, tile_pairs, tile_count, near_a, near_b, parts, mine)

    z, w, pay, mw, cr = call(
        functools.partial(first_kernel, subs),
        [vec, vec, row, vec, line],
        raw=[kernel_tiles],
        scratch=sweeping,
        smem=1,
    )(me, got, g_lines, zb, aggs, res, fine)
    x, r = res, res
    old = ()
    for iteration in range(ITERS):
        first, last = iteration == 0, iteration == ITERS - 1
        got = lax.all_to_all(pay, AXES, 0, 0, tiled=True)
        state = (z, w, x, r, cr, mw, zb, aggs, g_lines)
        body = functools.partial(step_kernel, subs, first, last, iteration == ITERS - 2)
        if last:
            outs = [vec, vec, vec, vec, small, small, line, ((subs, 128), F32)]
            room = [pltpu.VMEM((fields, span + 256), F32)]
            run = call(body, outs, scratch=room, smem=1)
            x, r, d, z, rz, fine_rz, _, pay = run(me, got, *state, *old, coarse_noise)
        else:
            outs = [vec] * 4 + [small, small, line, win, line, win, vec, vec, vec, row]
            run = call(body, outs, raw=[kernel_tiles], scratch=sweeping, smem=1)
            x, r, d, q, rz, curve, crq, mq, cr, zb, z, w, mw, pay = run(
                me, got, *neighbours(mw), *state, *old, fine
            )
            old = (rz, curve, d, q, crq, mq)
    coarse_rz = lax.all_to_all(pay, "sub", 0, 0, tiled=True)
    (d,) = call(last_kernel, [vec])(coarse_rz, z, d, rz, fine_rz)
    return (x, r, d)


def solution(mesh):
    devices = mesh.devices
    blk, subs = devices.shape
    fine_mesh = Mesh(devices.reshape(blk // CORES, CORES, subs), AXES)
    points = P(None, AXES)
    in_specs = (
        points,
        points,
        points,
        P(AXES),
        P(AXES, None, None),
        P("sub", None),
        P(AXES),
    )
    return jax.shard_map(
        per_device, mesh=fine_mesh, in_specs=in_specs, out_specs=(points,) * 3, check_vma=False
    )
```
